512 devices in a mesh: req: 128 (over x_lo, z, y), tp: 4 (over x_hi, core).
Axes of the slice: x: 4 (x_hi: 2, x_lo: 2; x = x_hi * 2 + x_lo), y: 4, z: 16, core: 2. Of those that a mesh axis runs over, the one named last changes fastest.
Arguments:
- q_pre: bfloat16 [65536, 1024], P(('req', 'tp')), may hold values from -6 to 6
- gate_pre: bfloat16 [65536, 8], P(('req', 'tp')), may hold values from -6 to 6
- k_pre: bfloat16 [65536, 512], P(('req', 'tp')), may hold values from -6 to 6
- v_pre: bfloat16 [65536, 512], P(('req', 'tp')), may hold values from -6 to 6
- q_gain: float32 [128], replicated, may hold values from 0.1 to 1.9
- k_gain: float32 [128], replicated, may hold values from 0.1 to 1.9
- lengths: int32 [128, 3], P('req'), may hold values from 1 to 256, 512 in all within a row
- q_new: bfloat16 [384, 1024], P('req'), may hold values from -6 to 6
- gate_new: bfloat16 [384, 8], P('req'), may hold values from -6 to 6
- k_new: bfloat16 [384, 512], P('req'), may hold values from -6 to 6
- v_new: bfloat16 [384, 512], P('req'), may hold values from -6 to 6
- resid: bfloat16 [384, 2048], P('req'), may hold values from -5 to 5
- w_out: bfloat16 [1024, 2048], P('tp'), may hold values from -0.1875 to 0.1875
- norm_gain: float32 [2048], replicated, may hold values from 0.1 to 1.9
- w_gate: bfloat16 [2048, 3072], P('req', 'tp'), may hold values from -0.125 to 0.125
- w_up: bfloat16 [2048, 3072], P('req', 'tp'), may hold values from -0.125 to 0.125
- w_down: bfloat16 [3072, 2048], P('tp', 'req'), may hold values from -0.109375 to 0.109375
Outputs:
- prefill_out: bfloat16 [65536, 1024], P(('req', 'tp'))
- decode_out: bfloat16 [384, 2048], P('req')
The draws below stay inside these ranges and needn't reach their ends.
Inputs may be any that keep to these rules, and one draw needn't show every extreme that they name: Each row holds the prompt lengths of one group's 3 requests; they sum to 512 and the longest is exactly 256.
All inputs are finite; a program needn't handle non-finite values.
Results may differ from the reference program's by a relative error of at most 0.0065.
Values may be sent and summed in bfloat16 or wider, within the bound.
A program may use at most 64 MiB of HBM per device.

```python
import math
import jax
import jax.numpy as jnp
import numpy as np
from jax import lax

D = 2048
FF = 3072
HD = 128
Q_HEADS = 8
KV_HEADS = 4
SEQ = 512
MAX_LEN = 256
RPG = 3
TOKENS = 65536
REQUESTS = 384
N_REQ = 128


def block_scale(own_key, shape, shards, least, top_value):
    level = 1.0
    for dim, shards_of in shards:
        draws = jax.random.uniform(jax.random.fold_in(jax.random.fold_in(own_key, 6), dim), (shards_of,), jnp.float32, least / len(shards), top_value / len(shards))
        level = level * jnp.repeat(jnp.exp(draws), shape[dim] // shards_of).reshape((-1,) + (1,) * (len(shape) - 1 - dim))
    return level


def split_up(number_of, total, bound, slope):
    weights = [(1 << 20) // math.isqrt(grade ** slope) + 1 for grade in range(2, number_of + 1)]
    rest, given = total - bound - (number_of - 1), [1] * (number_of - 1)
    while rest > 0:
        movable = [i for i in range(number_of - 1) if given[i] < bound]
        whole, remaining = sum([weights[i] for i in movable]), rest
        for i in movable:
            more = min(bound - given[i], max(1, remaining * weights[i] // whole), rest)
            given[i] = given[i] + more
            rest = rest - more
    return np.array([bound] + given)


def uneven_parts(key, count, total, limit, skew):
    if count == 2:
        one = jax.random.randint(key, (), max(1, total - limit), min(limit, total - 1) + 1)
        return jnp.stack([one, total - one])
    sizes = jnp.asarray(split_up(count, total, limit, skew), jnp.int32)
    pairs = (count - 1) // 2
    source_of, taker = sizes[1:1 + 2 * pairs:2], sizes[2:2 + 2 * pairs:2]
    margin = jnp.minimum(source_of - 1, limit - taker)
    moved = jax.random.randint(jax.random.fold_in(key, 1), (pairs,), 0, 1 << 20) % (margin + 1)
    sizes = sizes.at[1:1 + 2 * pairs:2].set(source_of - moved).at[2:2 + 2 * pairs:2].set(taker + moved)
    return sizes[jax.random.permutation(jax.random.fold_in(key, 2), count)]


def normal_values(own_key, shape, spread, reach, split=(), kind=jnp.bfloat16):
    entries = spread * jax.random.normal(own_key, shape, jnp.float32)
    if split:
        entries = entries * block_scale(own_key, shape, split, -0.22, 0.18)
    return jnp.clip(entries, -reach, reach).astype(kind)


def setup_inputs(seed: int = 0) -> dict:
    streams_of = jax.random.split(jax.random.key(seed), 18)
    return {
        "q_pre": normal_values(streams_of[0], (TOKENS, Q_HEADS * HD), 1.0, 6.0, ((0, 512),)),
        "gate_pre": normal_values(streams_of[1], (TOKENS, Q_HEADS), 1.5, 6.0, ((0, 512),)),
        "k_pre": normal_values(streams_of[2], (TOKENS, KV_HEADS * HD), 1.0, 6.0, ((0, 512),)),
        "v_pre": normal_values(streams_of[3], (TOKENS, KV_HEADS * HD), 1.0, 6.0, ((0, 512),)),
        "q_gain": jnp.clip(1.0 + 0.18 * jax.random.normal(streams_of[4], (HD,), jnp.float32), 0.1, 1.9),
        "k_gain": jnp.clip(1.0 + 0.18 * jax.random.normal(streams_of[5], (HD,), jnp.float32), 0.1, 1.9),
        "lengths": jax.vmap(lambda own: uneven_parts(own, RPG, SEQ, MAX_LEN, 2))(jax.random.split(streams_of[6], N_REQ)).reshape((N_REQ, RPG)).astype(jnp.int32),
        "q_new": normal_values(streams_of[7], (REQUESTS, Q_HEADS * HD), 1.0, 6.0, ((0, 128),)),
        "gate_new": normal_values(streams_of[8], (REQUESTS, Q_HEADS), 1.5, 6.0, ((0, 128),)),
        "k_new": normal_values(streams_of[9], (REQUESTS, KV_HEADS * HD), 1.0, 6.0, ((0, 128),)),
        "v_new": normal_values(streams_of[10], (REQUESTS, KV_HEADS * HD), 1.0, 6.0, ((0, 128),)),
        "resid": normal_values(streams_of[11], (REQUESTS, D), 0.7, 5.0, ((0, 128),)),
        "w_out": normal_values(streams_of[12], (Q_HEADS * HD, D), (Q_HEADS * HD) ** -0.5, 0.1875, ((0, 4),)),
        "norm_gain": jnp.clip(1.0 + 0.18 * jax.random.normal(streams_of[13], (D,), jnp.float32), 0.1, 1.9),
        "w_gate": normal_values(streams_of[14], (D, FF), D ** -0.5, 0.125, ((0, 128), (1, 4))),
        "w_up": normal_values(streams_of[15], (D, FF), D ** -0.5, 0.125, ((0, 128), (1, 4))),
        "w_down": normal_values(streams_of[16], (FF, D), FF ** -0.5, 0.109375, ((0, 4), (1, 128))),
    }


rope_base = 1000000.0
norm_eps = 1e-06

def group_layout(lengths_row, total):
    req_ends = jnp.cumsum(lengths_row).astype(jnp.int32)
    req_starts = (req_ends - lengths_row).astype(jnp.int32)
    indices = jnp.arange(total, dtype=jnp.int32)
    segment = lax.optimization_barrier(jnp.sum((indices[:, None] >= req_ends[None, :]).astype(jnp.int32), axis=1)).astype(jnp.int32)
    onehot = segment[:, None] == jnp.arange(lengths_row.shape[0], dtype=jnp.int32)[None, :]
    offsets = lax.optimization_barrier(jnp.sum(jnp.where(onehot, req_starts[None, :], 0), axis=1)).astype(jnp.int32)
    return (segment, (indices - offsets).astype(jnp.int32))

def head_norm(values, gain):
    mean_sq = lax.optimization_barrier(jnp.mean(values * values, axis=-1, keepdims=True))
    return values * lax.rsqrt(mean_sq + norm_eps) * gain

def rotate(values, position):
    half_size = values.shape[-1] // 2
    freqs = rope_base ** (-(jnp.arange(half_size, dtype=jnp.float32) * 2.0 / (2 * half_size)))
    angles = position.astype(jnp.float32)[:, None] * freqs[None, :]
    shaped = (values.shape[0],) + (1,) * (values.ndim - 2) + (half_size,)
    cosine = jnp.cos(angles).reshape(shaped)
    sine = jnp.sin(angles).reshape(shaped)
    first_half = values[..., :half_size]
    second_half = values[..., half_size:]
    return jnp.concatenate([first_half * cosine - second_half * sine, second_half * cosine + first_half * sine], axis=-1)

def reference(q_pre, gate_pre, k_pre, v_pre, q_gain, k_gain, lengths, q_new, gate_new, k_new, v_new, resid, w_out, norm_gain, w_gate, w_up, w_down):
    groups_per = Q_HEADS // KV_HEADS
    score_scale = HD ** (-0.5)

    def one_group(inputs):
        q_grp, g_grp, k_grp, v_grp, lengths_row, qn_grp, gn_grp, kn_grp, vn_grp = inputs
        segment, position = group_layout(lengths_row, SEQ)
        indices = jnp.arange(SEQ, dtype=jnp.int32)
        queries = rotate(head_norm(q_grp.reshape(SEQ, Q_HEADS, HD).astype(jnp.float32), q_gain), position).astype(jnp.bfloat16)
        keys = rotate(head_norm(k_grp.reshape(SEQ, KV_HEADS, HD).astype(jnp.float32), k_gain), position).astype(jnp.bfloat16)
        values = v_grp.reshape(SEQ, KV_HEADS, HD).astype(jnp.float32)
        query_f = lax.optimization_barrier(queries).astype(jnp.float32).reshape(SEQ, KV_HEADS, groups_per, HD)
        key_f = lax.optimization_barrier(keys).astype(jnp.float32)
        scores = jnp.einsum('qkgd,pkd->qkgp', query_f, key_f) * score_scale
        allowed = (segment[:, None] == segment[None, :]) & (indices[:, None] >= indices[None, :])
        weights = jnp.where(allowed[:, None, None, :], jnp.exp(scores), 0.0)
        totals = lax.optimization_barrier(jnp.sum(weights, axis=-1))
        rounded = lax.optimization_barrier(weights.astype(jnp.bfloat16)).astype(jnp.float32)
        mixed = jnp.einsum('qkgp,pkd->qkgd', rounded, values)
        gates = jax.nn.sigmoid(g_grp.astype(jnp.float32)).reshape(SEQ, KV_HEADS, groups_per)
        prefill = (mixed / totals[..., None] * gates[..., None]).astype(jnp.bfloat16).reshape(SEQ, Q_HEADS * HD)
        new_queries = rotate(head_norm(qn_grp.reshape(RPG, Q_HEADS, HD).astype(jnp.float32), q_gain), lengths_row).astype(jnp.bfloat16)
        new_keys = rotate(head_norm(kn_grp.reshape(RPG, KV_HEADS, HD).astype(jnp.float32), k_gain), lengths_row).astype(jnp.bfloat16)
        nq_f = lax.optimization_barrier(new_queries).astype(jnp.float32).reshape(RPG, KV_HEADS, groups_per, HD)
        nk_f = lax.optimization_barrier(new_keys).astype(jnp.float32)
        cache_scores = jnp.einsum('rkgd,pkd->rkgp', nq_f, key_f) * score_scale
        owned = segment[None, :] == jnp.arange(RPG, dtype=jnp.int32)[:, None]
        cache_weights = jnp.where(owned[:, None, None, :], jnp.exp(cache_scores), 0.0)
        self_weight = jnp.exp(jnp.einsum('rkgd,rkd->rkg', nq_f, nk_f) * score_scale)
        dec_totals = lax.optimization_barrier(jnp.sum(cache_weights, axis=-1)) + self_weight
        cache_rounded = lax.optimization_barrier(cache_weights.astype(jnp.bfloat16)).astype(jnp.float32)
        dec_mixed = jnp.einsum('rkgp,pkd->rkgd', cache_rounded, values)
        dec_mixed = dec_mixed + self_weight[..., None] * vn_grp.reshape(RPG, KV_HEADS, 1, HD).astype(jnp.float32)
        dec_gates = jax.nn.sigmoid(gn_grp.astype(jnp.float32)).reshape(RPG, KV_HEADS, groups_per)
        decoded = (dec_mixed / dec_totals[..., None] * dec_gates[..., None]).astype(jnp.bfloat16).reshape(RPG, Q_HEADS * HD)
        return (prefill, decoded)
    prefill_all, decode_heads = lax.map(one_group, (q_pre.reshape(N_REQ, SEQ, Q_HEADS * HD), gate_pre.reshape(N_REQ, SEQ, Q_HEADS), k_pre.reshape(N_REQ, SEQ, KV_HEADS * HD), v_pre.reshape(N_REQ, SEQ, KV_HEADS * HD), lengths, q_new.reshape(N_REQ, RPG, Q_HEADS * HD), gate_new.reshape(N_REQ, RPG, Q_HEADS), k_new.reshape(N_REQ, RPG, KV_HEADS * HD), v_new.reshape(N_REQ, RPG, KV_HEADS * HD)))
    decode_heads = decode_heads.reshape(REQUESTS, Q_HEADS * HD)
    hidden_state = resid.astype(jnp.float32) + jnp.dot(decode_heads, w_out, preferred_element_type=jnp.float32)
    mean_sq = lax.optimization_barrier(jnp.mean(hidden_state * hidden_state, axis=-1, keepdims=True))
    normed = (hidden_state * lax.rsqrt(mean_sq + norm_eps) * norm_gain).astype(jnp.bfloat16)
    gate_part = jnp.dot(normed, w_gate, preferred_element_type=jnp.float32)
    up_part = jnp.dot(normed, w_up, preferred_element_type=jnp.float32)
    hidden_units = (jax.nn.silu(gate_part) * up_part).astype(jnp.bfloat16)
    decode_out = (hidden_state + jnp.dot(hidden_units, w_down, preferred_element_type=jnp.float32)).astype(jnp.bfloat16)
    return (prefill_all.reshape(TOKENS, Q_HEADS * HD), decode_out)
```

```python
import jax
import jax.numpy as jnp
from jax import lax
from jax.sharding import PartitionSpec as P

rope_base = 1000000.0
norm_eps = 1e-06
req = ("xlo", "z", "y")
tp = ("xhi", "core")


def group_layout(lengths_row, total):
    req_ends = jnp.cumsum(lengths_row)
    req_starts = req_ends - lengths_row
    indices = jnp.arange(total, dtype=jnp.int32)
    segment = jnp.sum((indices[:, None] >= req_ends[None, :]).astype(jnp.int32), axis=1)
    onehot = segment[:, None] == jnp.arange(lengths_row.shape[0], dtype=jnp.int32)[None, :]
    offsets = jnp.sum(jnp.where(onehot, req_starts[None, :], 0), axis=1)
    return (segment, indices - offsets)


def head_norm(values, gain):
    mean_sq = jnp.mean(values * values, axis=-1, keepdims=True)
    return values * lax.rsqrt(mean_sq + norm_eps) * gain


def rotate(values, position):
    half_size = values.shape[-1] // 2
    freqs = rope_base ** (-(jnp.arange(half_size, dtype=jnp.float32) * 2.0 / (2 * half_size)))
    angles = position.astype(jnp.float32)[:, None] * freqs[None, :]
    shaped = (values.shape[0],) + (1,) * (values.ndim - 2) + (half_size,)
    cosine = jnp.cos(angles).reshape(shaped)
    sine = jnp.sin(angles).reshape(shaped)
    first_half = values[..., :half_size]
    second_half = values[..., half_size:]
    return jnp.concatenate(
        [first_half * cosine - second_half * sine, second_half * cosine + first_half * sine],
        axis=-1,
    )


def local(
    q_pre,
    gate_pre,
    k_pre,
    v_pre,
    q_gain,
    k_gain,
    lengths,
    q_new,
    gate_new,
    k_new,
    v_new,
    resid,
    w_out,
    norm_gain,
    w_gate,
    w_up,
    w_down,
):
    tok_rows = q_pre.shape[0]
    tp_count = lax.axis_size(tp)
    tp_index = lax.axis_index(tp)
    head_size = q_gain.shape[0]
    query_heads = gate_pre.shape[1]
    kv_heads = k_pre.shape[1] // head_size
    groups_per = query_heads // kv_heads
    kv_local = kv_heads // tp_count
    req_count = lengths.shape[1]
    score_scale = head_size ** (-0.5)
    segment, position = group_layout(lengths[0], tok_rows * tp_count)
    row_offset = tp_index * tok_rows
    seg_local = lax.dynamic_slice_in_dim(segment, row_offset, tok_rows)
    pos_local = lax.dynamic_slice_in_dim(position, row_offset, tok_rows)
    query_index = row_offset + jnp.arange(tok_rows, dtype=jnp.int32)
    queries = rotate(
        head_norm(q_pre.reshape(tok_rows, query_heads, head_size).astype(jnp.float32), q_gain),
        pos_local,
    )
    queries = queries.astype(jnp.bfloat16).reshape(tok_rows, kv_heads, groups_per, head_size)
    keys = rotate(
        head_norm(k_pre.reshape(tok_rows, kv_heads, head_size).astype(jnp.float32), k_gain),
        pos_local,
    ).astype(jnp.bfloat16)
    values = v_pre.reshape(tok_rows, kv_heads, head_size)

    def key_block(running, key_piece, value_piece, first_row):
        key_count = key_piece.shape[0]
        key_index = first_row + jnp.arange(key_count, dtype=jnp.int32)
        allowed = (seg_local[:, None] == segment[None, :]) & (
            query_index[:, None] >= key_index[None, :]
        )
        scores = (
            jnp.einsum(
                "qkgd,pkd->qkgp",
                queries,
                key_piece.reshape(key_count, kv_heads, head_size),
                preferred_element_type=jnp.float32,
            )
            * score_scale
        )
        weights = jnp.where(allowed[:, None, None, :], jnp.exp(scores), 0.0)
        totals = running[0] + jnp.sum(weights, axis=-1)
        mixed = running[1] + jnp.einsum(
            "qkgp,pkd->qkgd",
            weights.astype(jnp.bfloat16),
            value_piece.reshape(key_count, kv_heads, head_size),
            preferred_element_type=jnp.float32,
        )
        return (totals, mixed)

    start_state = (
        jnp.zeros((tok_rows, kv_heads, groups_per), jnp.float32),
        jnp.zeros((tok_rows, kv_heads, groups_per, head_size), jnp.float32),
    )
    pieces = (
        lax.all_gather(keys.reshape(tok_rows, kv_heads * head_size), tp, axis=0, tiled=True),
        lax.all_gather(v_pre, tp, axis=0, tiled=True),
    )
    key_count = pieces[0].shape[0]
    block_rows = 512

    def one_block(number, carried):
        begin_at = number * block_rows
        return key_block(carried, pieces[0], pieces[1], begin_at)

    totals, mixed = lax.fori_loop(0, key_count // block_rows, one_block, start_state)
    gates = jax.nn.sigmoid(gate_pre.astype(jnp.float32)).reshape(tok_rows, kv_heads, groups_per)
    prefill_out = (
        (mixed / totals[..., None] * gates[..., None])
        .astype(jnp.bfloat16)
        .reshape(tok_rows, query_heads * head_size)
    )
    new_queries = rotate(
        head_norm(q_new.reshape(req_count, query_heads, head_size).astype(jnp.float32), q_gain),
        lengths[0],
    )
    new_queries = new_queries.astype(jnp.bfloat16).reshape(
        req_count, kv_heads, groups_per, head_size
    )
    new_keys = rotate(
        head_norm(k_new.reshape(req_count, kv_heads, head_size).astype(jnp.float32), k_gain),
        lengths[0],
    ).astype(jnp.bfloat16)
    new_values = v_new.reshape(req_count, kv_heads, head_size)
    new_gates = jax.nn.sigmoid(gate_new.astype(jnp.float32)).reshape(
        req_count, kv_heads, groups_per
    )
    request_ids = jnp.arange(req_count, dtype=jnp.int32)
    dec_scores = (
        jnp.einsum("rkgd,pkd->rkgp", new_queries, keys, preferred_element_type=jnp.float32)
        * score_scale
    )
    owned = seg_local[None, :] == request_ids[:, None]
    dec_weights = jnp.where(owned[:, None, None, :], jnp.exp(dec_scores), 0.0)
    dec_part = jnp.einsum(
        "rkgp,pkd->rkgd",
        dec_weights.astype(jnp.bfloat16),
        values,
        preferred_element_type=jnp.float32,
    )
    dec_sum = jnp.sum(dec_weights, axis=-1, keepdims=True)
    both = jnp.concatenate([dec_part, jnp.broadcast_to(dec_sum, dec_part.shape)], axis=0)
    both = lax.psum(both, tp)
    head_first = tp_index * kv_local
    both = lax.dynamic_slice_in_dim(both, head_first, kv_local, 1)
    dec_mixed, dec_totals = both[:req_count], both[req_count:, ..., 0]
    own_queries = lax.dynamic_slice_in_dim(new_queries, head_first, kv_local, 1)
    own_keys = lax.dynamic_slice_in_dim(new_keys, head_first, kv_local, 1)
    own_values = lax.dynamic_slice_in_dim(new_values, head_first, kv_local, 1)
    own_gates = lax.dynamic_slice_in_dim(new_gates, head_first, kv_local, 1)
    self_weight = jnp.exp(
        jnp.einsum("rkgd,rkd->rkg", own_queries, own_keys, preferred_element_type=jnp.float32)
        * score_scale
    )
    dec_totals = dec_totals + self_weight
    dec_mixed = dec_mixed + self_weight[..., None] * own_values.astype(jnp.float32)[:, :, None, :]
    attended = (
        (dec_mixed / dec_totals[..., None] * own_gates[..., None])
        .astype(jnp.bfloat16)
        .reshape(req_count, kv_local * groups_per * head_size)
    )
    partial_out = jnp.dot(attended, w_out, preferred_element_type=jnp.float32)
    attn_rows = lax.psum(partial_out, tp)
    hidden_state = resid.astype(jnp.float32) + attn_rows
    mean_sq = jnp.mean(hidden_state * hidden_state, axis=-1, keepdims=True)
    normed = (hidden_state * lax.rsqrt(mean_sq + norm_eps) * norm_gain).astype(jnp.bfloat16)
    width = normed.shape[1]
    rows_each = w_gate.shape[0]
    nx, nz, ny = lax.axis_size("xlo"), lax.axis_size("z"), lax.axis_size("y")
    stacked = jnp.concatenate([w_gate, w_up, w_down.T], axis=1)
    gathered = lax.all_gather(stacked, "z", axis=0, tiled=True)
    units_local = w_gate.shape[1]
    plane = lax.all_gather(normed, ("xlo", "y"), axis=0, tiled=True)
    plane = plane.reshape(-1, nx, nz, ny, rows_each)
    plane = lax.dynamic_index_in_dim(plane, lax.axis_index("xlo"), 1, keepdims=False)
    plane = lax.dynamic_index_in_dim(plane, lax.axis_index("y"), 2, keepdims=False)
    columns = plane.reshape(plane.shape[0], nz * rows_each)
    sums = lax.psum(
        jnp.dot(columns, gathered[:, : 2 * units_local], preferred_element_type=jnp.float32),
        ("xlo", "y"),
    )
    hidden_units = (jax.nn.silu(sums[:, :units_local]) * sums[:, units_local:]).astype(jnp.bfloat16)
    down_part = lax.dot_general(
        hidden_units,
        gathered[:, 2 * units_local :],
        (((1,), (1,)), ((), ())),
        preferred_element_type=jnp.float32,
    )
    down_part = lax.psum(down_part, tp)
    back = lax.all_gather(down_part, ("xlo", "y"), axis=0, tiled=False)
    group = lax.axis_index(("xlo", "y"))
    back = lax.dynamic_slice_in_dim(back, group * req_count, req_count, 1)
    back = back.reshape(nx, ny, req_count, nz, rows_each).transpose(2, 0, 3, 1, 4)
    mlp_rows = back.reshape(req_count, width)
    decode_out = (hidden_state + mlp_rows).astype(jnp.bfloat16)
    return (prefill_out, decode_out)


def solution(mesh):
    wide = jax.sharding.Mesh(
        mesh.devices.reshape(2, 16, 4, 2, 2), ("xlo", "z", "y", "xhi", "core")
    )
    return jax.shard_map(
        local,
        mesh=wide,
        in_specs=(
            P(req + tp, None),
            P(req + tp, None),
            P(req + tp, None),
            P(req + tp, None),
            P(),
            P(),
            P(req, None),
            P(req, None),
            P(req, None),
            P(req, None),
            P(req, None),
            P(req, None),
            P(tp, None),
            P(),
            P(req, tp),
            P(req, tp),
            P(tp, req),
        ),
        out_specs=(P(req + tp, None), P(req, None)),
        check_vma=False,
    )
```

```python
import functools

import jax
import jax.numpy as jnp
from jax import lax
from jax.experimental import pallas as pl
from jax.experimental.pallas import tpu as pltpu
from jax.sharding import PartitionSpec as P

rope_base = 1000000.0
norm_eps = 1e-06
req = ("xlo", "z", "y")
tp = ("xhi", "core")
NX, NZ, NY, NT = 2, 16, 4, 4
NP = NX * NY
HD = 128
HEADS = 8
KVH = 4
TOK = 128
CHUNK = 96
MASKED = -1e30
f32 = jnp.float32
bf16 = jnp.bfloat16


def iota(shape, dim):
    return lax.broadcasted_iota(jnp.int32, shape, dim)


def roll(values, shift, axis):
    return pltpu.roll(values, shift, axis)


def nt_dot(a, b):
    return lax.dot_general(a, b, (((1,), (1,)), ((), ())), preferred_element_type=f32)


def rope_tables(position):
    lane = iota(position.shape, 1)
    index = (lane % 64).astype(f32)
    freqs = jnp.exp(index * (-2.0 / HD * 13.815510557964274))
    angles = position * freqs
    sine = jnp.sin(angles)
    return jnp.cos(angles), jnp.where(lane < 64, -sine, sine)


def norm_rope(values, gain, cosine, sine):
    mean_sq = jnp.mean(values * values, axis=-1, keepdims=True)
    normed = values * lax.rsqrt(mean_sq + norm_eps) * gain
    return normed * cosine + roll(normed, 64, 1) * sine


def swap_halves(values):
    keep = (iota((8, 128), 0) < 4) == (iota((8, 128), 1) < 64)
    tiles = []
    for j in range(values.shape[1] // 128):
        tile = values[:, j * 128 : (j + 1) * 128]
        tiles.append(jnp.where(keep, tile, roll(roll(tile, 64, 1), 4, 0)))
    return jnp.concatenate(tiles, axis=1)


def kernel(
    lengths_ref,
    q_ref,
    gate_ref,
    k_ref,
    v_ref,
    qg_ref,
    kg_ref,
    qn_ref,
    gn_ref,
    kn_ref,
    vn_ref,
    resid_ref,
    wo_ref,
    ng_ref,
    wg_ref,
    wu_ref,
    wd_ref,
    out_ref,
    dec_ref,
    keys,
    vals,
    bias,
    nq,
    nk,
    nv,
    ngate,
    selfw,
    fold,
    piece_out,
    piece_in,
    gathered,
    x1_out,
    x1_in,
    x2,
    xa,
    xb_out,
    xb_in,
    xc,
    cos_t,
    sin_t,
    gates,
    s1_send,
    s1_recv,
    kv_send,
    kv_recv,
    x1_send,
    x1_recv,
    x2_send,
    x2_recv,
    xa_send,
    xa_recv,
    xb_send,
    xb_recv,
    xc_send,
    xc_recv,
    right_send,
    right_recv,
    left_send,
    left_recv,
):
    xlo, z, y = lax.axis_index("xlo"), lax.axis_index("z"), lax.axis_index("y")
    t = lax.axis_index("xhi") * 2 + lax.axis_index("core")
    p = xlo * NY + y

    def tp_dev(i):
        return {"xhi": i // 2, "core": i % 2}

    def plane_dev(i):
        return {"xlo": i // NY, "y": i % NY}

    def z_dev(i):
        return {"z": i % NZ}

    barrier = pltpu.get_barrier_semaphore()
    mesh_id = pl.DeviceIdType.MESH
    for d in range(1, NT):
        pl.semaphore_signal(barrier, inc=1, device_id=tp_dev((t + d) % NT), device_id_type=mesh_id)
    for d in range(1, NP):
        pl.semaphore_signal(barrier, inc=1, device_id=plane_dev((p + d) % NP), device_id_type=mesh_id)
    pl.semaphore_signal(barrier, inc=1, device_id=z_dev(z + 1), device_id_type=mesh_id)
    pl.semaphore_signal(barrier, inc=1, device_id=z_dev(z + NZ - 1), device_id_type=mesh_id)

    started = []

    def send(src, dst, send_sem, recv_sem, device):
        copy = pltpu.make_async_remote_copy(
            src_ref=src,
            dst_ref=dst,
            send_sem=send_sem,
            recv_sem=recv_sem,
            device_id=device,
            device_id_type=mesh_id,
        )
        copy.start()
        started.append(copy)
        return copy

    for n, ref in enumerate((wg_ref, wu_ref, wd_ref)):
        whole = ref[...].astype(f32)
        width = whole.shape[1]
        for i in range(NP):
            part = whole if i == 0 else roll(whole, width - CHUNK * i, 1)
            piece_out[i, :, n * 128 : (n + 1) * 128] = part[:, :128].astype(bf16)
    piece_in[pl.ds(p, 1)] = piece_out[pl.ds(p, 1)]

    pl.semaphore_wait(barrier, NT - 1 + NP - 1 + 2)
    s1 = [
        send(piece_out.at[(p + d) % NP], piece_in.at[p], s1_send.at[d - 1], s1_recv.at[d - 1], plane_dev((p + d) % NP))
        for d in range(1, NP)
    ]

    len0, len1, len2 = lengths_ref[0, 0], lengths_ref[0, 1], lengths_ref[0, 2]
    end0, end1 = len0, len0 + len1
    end2 = end1 + len2

    def start_of(index):
        return jnp.where(index >= end1, end1, jnp.where(index >= end0, end0, 0))

    own_index = t * TOK + iota((TOK, 128), 0)
    cosine, sine = rope_tables((own_index - start_of(own_index)).astype(f32))
    cos_t[...] = cosine
    sin_t[...] = sine

    k_gain = kg_ref[...]
    q_gain = qg_ref[...]
    for k in range(KVH):
        lanes = slice(k * HD, (k + 1) * HD)
        keys[2, :, lanes] = norm_rope(k_ref[:, lanes].astype(f32), k_gain, cosine, sine).astype(bf16)
    for d in (1, 2):

        @pl.when(t + d < NT)
        def _(d=d):
            for n, (src, dst) in enumerate(((keys.at[2], keys.at[2 - d]), (v_ref, vals.at[2 - d]))):
                pltpu.make_async_remote_copy(
                    src_ref=src,
                    dst_ref=dst,
                    send_sem=kv_send.at[d - 1, n],
                    recv_sem=kv_recv.at[d - 1, n],
                    device_id=tp_dev(lax.rem(t + d, NT)),
                    device_id_type=mesh_id,
                ).start()

        @pl.when(t < d)
        def _(d=d):
            keys[2 - d] = jnp.zeros((TOK, KVH * HD), bf16)
            vals[2 - d] = jnp.zeros((TOK, KVH * HD), bf16)

    for ref in (nq, nk, nv, ngate):
        ref[...] = jnp.zeros_like(ref)
    for h in range(HEADS):
        rows = slice(h * 4, h * 4 + 3)
        lanes = slice(h * HD, (h + 1) * HD)
        kv_lanes = slice(h // 2 * HD, (h // 2 + 1) * HD)
        nq[rows, :] = qn_ref[:, lanes].astype(f32)
        nk[rows, :] = kn_ref[:, kv_lanes].astype(f32)
        nv[rows, :] = vn_ref[:, kv_lanes].astype(f32)
        ngate[rows, :] = jnp.broadcast_to(gn_ref[:, h : h + 1].astype(f32), (3, HD))
    request = iota((HEADS * 4, HD), 0) % 4
    new_pos = jnp.where(request == 0, len0, jnp.where(request == 1, len1, jnp.where(request == 2, len2, 0)))
    new_cos, new_sin = rope_tables(new_pos.astype(f32))
    scale = HD**-0.5
    new_q = norm_rope(nq[...], q_gain, new_cos, new_sin).astype(bf16)
    new_k = norm_rope(nk[...], k_gain, new_cos, new_sin).astype(bf16)
    self_score = jnp.sum(new_q.astype(f32) * new_k.astype(f32), axis=-1, keepdims=True) * scale
    selfw[...] = jnp.broadcast_to(jnp.exp(self_score), selfw.shape)
    nq[...] = new_q.astype(f32)

    row_req = iota((8, TOK), 0) % 4
    token = t * TOK + iota((8, TOK), 1)
    begin = jnp.where(row_req == 0, 0, jnp.where(row_req == 1, end0, jnp.where(row_req == 2, end1, 0)))
    finish = jnp.where(row_req == 0, end0, jnp.where(row_req == 1, end1, jnp.where(row_req == 2, end2, 0)))
    own_bias = jnp.where((token >= begin) & (token < finish), 0.0, MASKED)
    for k in range(KVH):
        lanes = slice(k * HD, (k + 1) * HD)
        scores = nt_dot(nq[k * 8 : (k + 1) * 8, :].astype(bf16), keys[2, :, lanes]) * scale
        weights = jnp.exp(scores + own_bias)
        x1_out[k, 0:8, :] = jnp.dot(weights.astype(bf16), v_ref[:, lanes], preferred_element_type=f32)
        x1_out[k, 8:16, :] = jnp.broadcast_to(jnp.sum(weights, axis=-1, keepdims=True), (8, HD))
    x1_in[pl.ds(t, 1)] = x1_out[pl.ds(t, 1)]
    c1 = [
        send(x1_out.at[(t + d) % NT], x1_in.at[t], x1_send.at[d - 1], x1_recv.at[d - 1], tp_dev((t + d) % NT))
        for d in range(1, NT)
    ]

    for copy in s1:
        copy.wait_recv()
    block = piece_in[...].reshape(NP * 16, 3 * 128).astype(f32)
    for n in range(3):
        turned = jnp.transpose(block[:, n * 128 : (n + 1) * 128])
        gathered[pl.ds(z, 1), n * CHUNK : (n + 1) * CHUNK, :] = turned[:CHUNK, :].astype(bf16)[None]

    ring = {}

    def ring_step(s):
        if s > 1:
            for copy in ring[s - 1]:
                copy.wait_recv()
        if s > NZ // 2:
            return
        copies = []
        slot = gathered.at[(z + NZ - s + 1) % NZ]
        copies.append(send(slot, slot, right_send.at[s - 1], right_recv.at[s - 1], z_dev(z + 1)))
        if s < NZ // 2:
            slot = gathered.at[(z + s - 1) % NZ]
            copies.append(send(slot, slot, left_send.at[s - 1], left_recv.at[s - 1], z_dev(z + NZ - 1)))
        ring[s] = copies

    ring_step(1)

    low = iota((8, 1024), 0) < 4
    fold[...] = jnp.zeros_like(fold)
    fold[0:3, :] = resid_ref[:, :1024].astype(f32)
    fold[4:7, :] = resid_ref[:, 1024:].astype(f32)
    key_index = (t - 2) * TOK + iota((TOK, 3 * TOK), 1)
    query_index = t * TOK + iota((TOK, 3 * TOK), 0)
    allowed = (key_index >= start_of(query_index)) & (key_index <= query_index)
    bias[...] = jnp.where(allowed, 0.0, MASKED)
    gate_rows = jax.nn.sigmoid(gate_ref[...].astype(f32))
    gates[...] = jnp.transpose(jnp.concatenate([gate_rows, jnp.zeros((120, TOK), f32)], axis=0))

    for copy in c1:
        copy.wait_recv()
    both = x1_in[0] + x1_in[1] + x1_in[2] + x1_in[3]
    mine = pl.ds(pl.multiple_of(t * 8, 8), 8)
    own_self = selfw[mine, :]
    mixed = both[0:8] + own_self * nv[mine, :]
    attended = (mixed / (both[8:16] + own_self) * jax.nn.sigmoid(ngate[mine, :])).astype(bf16)
    first = jnp.dot(attended, wo_ref[0:HD, :], preferred_element_type=f32)
    second = jnp.dot(attended, wo_ref[HD : 2 * HD, :], preferred_element_type=f32)
    sums = first + roll(second, 4, 0)
    x2[pl.ds(t, 1)] = jnp.where(low, sums[:, :1024], roll(sums[:, 1024:], 4, 0))[None]
    c2 = [
        send(x2.at[t], x2.at[t], x2_send.at[d - 1], x2_recv.at[d - 1], tp_dev((t + d) % NT))
        for d in range(1, NT)
    ]
    ring_step(2)

    for d in (1, 2):

        @pl.when(t >= d)
        def _(d=d):
            for n, (src, dst) in enumerate(((keys.at[2], keys.at[2 - d]), (v_ref, vals.at[2 - d]))):
                pltpu.make_async_remote_copy(
                    src_ref=src,
                    dst_ref=dst,
                    send_sem=kv_send.at[d - 1, n],
                    recv_sem=kv_recv.at[d - 1, n],
                    device_id=tp_dev(lax.rem(t + d, NT)),
                    device_id_type=mesh_id,
                ).wait_recv()

    def attend(h):
        lanes = slice(h * HD, (h + 1) * HD)
        kv_lanes = slice(h // 2 * HD, (h // 2 + 1) * HD)
        query = norm_rope(q_ref[:, lanes].astype(f32), q_gain, cos_t[...], sin_t[...]).astype(bf16)
        total = jnp.zeros((TOK, 1), f32)
        mixed = jnp.zeros((TOK, HD), f32)
        for b in range(3):
            scores = nt_dot(query, keys[b, :, kv_lanes]) * scale
            weights = jnp.exp(scores + bias[:, b * TOK : (b + 1) * TOK])
            total = total + jnp.sum(weights, axis=-1, keepdims=True)
            value = v_ref[:, kv_lanes] if b == 2 else vals[b, :, kv_lanes]
            mixed = mixed + jnp.dot(weights.astype(bf16), value, preferred_element_type=f32)
        out_ref[:, lanes] = (mixed / total * gates[:, h : h + 1]).astype(bf16)

    attend(0)
    attend(1)

    for copy in c2:
        copy.wait_recv()
    hidden = fold[...] + (x2[0] + x2[1] + x2[2] + x2[3])
    squares = jnp.sum(hidden * hidden, axis=-1, keepdims=True)
    squares = jnp.broadcast_to(squares, (8, 128))
    mean_sq = ((squares + roll(squares, 4, 0)) / 2048.0)[:, 0:1]
    gain = jnp.where(low, ng_ref[:, :1024], ng_ref[:, 1024:])
    normed = (hidden * lax.rsqrt(mean_sq + norm_eps) * gain).astype(bf16).astype(f32)
    xa[pl.ds(p, 1)] = swap_halves(normed)[None]
    ca = [
        send(xa.at[p], xa.at[p], xa_send.at[d - 1], xa_recv.at[d - 1], plane_dev((p + d) % NP))
        for d in range(1, NP)
    ]
    for s in range(3, NZ // 2 + 2):
        ring_step(s)
        if s <= 5:
            attend(2 * s - 4)
            attend(2 * s - 3)

    for copy in ca:
        copy.wait_recv()
    tokens = xa[...].reshape(NP * 8, 1024).astype(bf16)
    parts = []
    for n in range(2):
        halves = []
        for h in range(2):
            total = jnp.zeros((NP * 8, CHUNK), f32)
            for j in range(NZ // 2):
                total = total + nt_dot(
                    tokens[:, j * 128 : (j + 1) * 128],
                    gathered[2 * j + h, n * CHUNK : (n + 1) * CHUNK, :],
                )
            halves.append(total)
        parts.append(halves)
    shift = NP * 8 - 4
    unit_gate = parts[0][0] + roll(jnp.concatenate([parts[0][1], jnp.zeros((NP * 8, 32), f32)], axis=1), shift, 0)[:, :CHUNK]
    unit_up = parts[1][0] + roll(jnp.concatenate([parts[1][1], jnp.zeros((NP * 8, 32), f32)], axis=1), shift, 0)[:, :CHUNK]
    units = (unit_gate / (1.0 + jnp.exp(-unit_gate)) * unit_up).astype(bf16)
    low_rows = iota((NP * 8, 128), 0) % 8 < 4
    for j in range(NZ // 2):
        even = jnp.dot(units, gathered[2 * j, 2 * CHUNK : 3 * CHUNK, :], preferred_element_type=f32)
        odd = jnp.dot(units, gathered[2 * j + 1, 2 * CHUNK : 3 * CHUNK, :], preferred_element_type=f32)
        xb_out[:, :, j * 128 : (j + 1) * 128] = jnp.where(low_rows, even, roll(odd, 4, 0)).reshape(NP, 8, 128)
    xb_in[pl.ds(p, 1)] = xb_out[pl.ds(p, 1)]
    cb = [
        send(xb_out.at[(p + d) % NP], xb_in.at[p], xb_send.at[d - 1], xb_recv.at[d - 1], plane_dev((p + d) % NP))
        for d in range(1, NP)
    ]
    for copy in cb:
        copy.wait_recv()
    total = xb_in[0]
    for i in range(1, NP):
        total = total + xb_in[i]
    xc[pl.ds(t, 1)] = total[None]
    cc = [
        send(xc.at[t], xc.at[t], xc_send.at[d - 1], xc_recv.at[d - 1], tp_dev((t + d) % NT))
        for d in range(1, NT)
    ]
    for copy in cc:
        copy.wait_recv()
    result = (hidden + swap_halves(xc[0] + xc[1] + xc[2] + xc[3])).astype(bf16)
    dec_ref[:, :1024] = result[0:3]
    dec_ref[:, 1024:] = result[4:7]

    for copy in started:
        copy.wait_send()
    for d in (1, 2):

        @pl.when(t + d < NT)
        def _(d=d):
            for n, (src, dst) in enumerate(((keys.at[2], keys.at[2 - d]), (v_ref, vals.at[2 - d]))):
                pltpu.make_async_remote_copy(
                    src_ref=src,
                    dst_ref=dst,
                    send_sem=kv_send.at[d - 1, n],
                    recv_sem=kv_recv.at[d - 1, n],
                    device_id=tp_dev(lax.rem(t + d, NT)),
                    device_id_type=mesh_id,
                ).wait_send()


def local(
    q_pre,
    gate_pre,
    k_pre,
    v_pre,
    q_gain,
    k_gain,
    lengths,
    q_new,
    gate_new,
    k_new,
    v_new,
    resid,
    w_out,
    norm_gain,
    w_gate,
    w_up,
    w_down,
):
    vmem = pl.BlockSpec(memory_space=pltpu.VMEM)
    dma = pltpu.SemaphoreType.DMA
    return pl.pallas_call(
        kernel,
        out_shape=(
            jax.ShapeDtypeStruct((TOK, HEADS * HD), bf16),
            jax.ShapeDtypeStruct((3, 2048), bf16),
        ),
        in_specs=[pl.BlockSpec(memory_space=pltpu.SMEM)] + [vmem] * 16,
        out_specs=(vmem, vmem),
        scratch_shapes=[
            pltpu.VMEM((3, TOK, KVH * HD), bf16),
            pltpu.VMEM((2, TOK, KVH * HD), bf16),
            pltpu.VMEM((TOK, 3 * TOK), f32),
            pltpu.VMEM((HEADS * 4, HD), f32),
            pltpu.VMEM((HEADS * 4, HD), f32),
            pltpu.VMEM((HEADS * 4, HD), f32),
            pltpu.VMEM((HEADS * 4, HD), f32),
            pltpu.VMEM((HEADS * 4, HD), f32),
            pltpu.VMEM((8, 1024), f32),
            pltpu.VMEM((NP, 16, 384), bf16),
            pltpu.VMEM((NP, 16, 384), bf16),
            pltpu.VMEM((NZ, 3 * CHUNK, 128), bf16),
            pltpu.VMEM((NT, 16, 128), f32),
            pltpu.VMEM((NT, 16, 128), f32),
            pltpu.VMEM((NT, 8, 1024), f32),
            pltpu.VMEM((NP, 8, 1024), f32),
            pltpu.VMEM((NP, 8, 1024), f32),
            pltpu.VMEM((NP, 8, 1024), f32),
            pltpu.VMEM((NT, 8, 1024), f32),
            pltpu.VMEM((TOK, HD), f32),
            pltpu.VMEM((TOK, HD), f32),
            pltpu.VMEM((TOK, 128), f32),
            dma((NP - 1,)),
            dma((NP - 1,)),
            dma((2, 2)),
            dma((2, 2)),
            dma((NT - 1,)),
            dma((NT - 1,)),
            dma((NT - 1,)),
            dma((NT - 1,)),
            dma((NP - 1,)),
            dma((NP - 1,)),
            dma((NP - 1,)),
            dma((NP - 1,)),
            dma((NT - 1,)),
            dma((NT - 1,)),
            dma((NZ // 2,)),
            dma((NZ // 2,)),
            dma((NZ // 2 - 1,)),
            dma((NZ // 2 - 1,)),
        ],
        compiler_params=pltpu.CompilerParams(
            collective_id=0, has_side_effects=True, vmem_limit_bytes=40 * 1024 * 1024
        ),
    )(
        lengths,
        q_pre,
        gate_pre.T,
        k_pre,
        v_pre,
        q_gain.reshape(1, HD),
        k_gain.reshape(1, HD),
        q_new,
        gate_new,
        k_new,
        v_new,
        resid,
        w_out,
        norm_gain.reshape(1, 2048),
        w_gate,
        w_up,
        w_down.T,
    )


def solution(mesh):
    wide = jax.sharding.Mesh(
        mesh.devices.reshape(NX, NZ, NY, 2, 2), ("xlo", "z", "y", "xhi", "core")
    )
    return jax.shard_map(
        local,
        mesh=wide,
        in_specs=(
            P(req + tp, None),
            P(req + tp, None),
            P(req + tp, None),
            P(req + tp, None),
            P(),
            P(),
            P(req, None),
            P(req, None),
            P(req, None),
            P(req, None),
            P(req, None),
            P(req, None),
            P(tp, None),
            P(),
            P(req, tp),
            P(req, tp),
            P(tp, req),
        ),
        out_specs=(P(req + tp, None), P(req, None)),
        check_vma=False,
    )
```

```python
import functools

import jax
import jax.numpy as jnp
from jax import lax
from jax.experimental import pallas as pl
from jax.experimental.pallas import tpu as pltpu
from jax.sharding import PartitionSpec as P

rope_base = 1000000.0
norm_eps = 1e-06
req = ("xlo", "z", "y")
tp = ("xhi", "core")
NX, NZ, NY, NT = 2, 16, 4, 4
NP = NX * NY
HD = 128
HEADS = 8
KVH = 4
TOK = 128
CHUNK = 96
CHUNKS = 2
ROWS = 3 * CHUNK // CHUNKS
MASKED = -1e30
f32 = jnp.float32
bf16 = jnp.bfloat16


def iota(shape, dim):
    return lax.broadcasted_iota(jnp.int32, shape, dim)


def roll(values, shift, axis):
    return pltpu.roll(values, shift, axis)


def nt_dot(a, b):
    return lax.dot_general(a, b, (((1,), (1,)), ((), ())), preferred_element_type=f32)


def rope_tables(position):
    lane = iota(position.shape, 1)
    index = (lane % 64).astype(f32)
    freqs = jnp.exp(index * (-2.0 / HD * 13.815510557964274))
    angles = position * freqs
    sine = jnp.sin(angles)
    return jnp.cos(angles), jnp.where(lane < 64, -sine, sine)


def norm_rope(values, gain, cosine, sine):
    mean_sq = jnp.mean(values * values, axis=-1, keepdims=True)
    normed = values * lax.rsqrt(mean_sq + norm_eps) * gain
    return normed * cosine + roll(normed, 64, 1) * sine


def swap_halves(values):
    keep = (iota((8, 128), 0) < 4) == (iota((8, 128), 1) < 64)
    tiles = []
    for j in range(values.shape[1] // 128):
        tile = values[:, j * 128 : (j + 1) * 128]
        tiles.append(jnp.where(keep, tile, roll(roll(tile, 64, 1), 4, 0)))
    return jnp.concatenate(tiles, axis=1)


def kernel(
    lengths_ref,
    q_hbm,
    gate_hbm,
    k_hbm,
    v_hbm,
    qg_hbm,
    kg_hbm,
    qn_hbm,
    gn_hbm,
    kn_hbm,
    vn_hbm,
    resid_hbm,
    wo_hbm,
    ng_hbm,
    wg_hbm,
    wu_hbm,
    wd_hbm,
    out_hbm,
    dec_hbm,
    keys,
    vals,
    bias,
    nq,
    nk,
    nv,
    ngate,
    selfw,
    fold,
    piece_out,
    piece_in,
    gathered,
    x1_out,
    x1_in,
    x2,
    xa,
    xb_out,
    xb_in,
    xc,
    cos_t,
    sin_t,
    gates,
    q_ref,
    gate_ref,
    k_ref,
    v_ref,
    qg_ref,
    kg_ref,
    qn_ref,
    gn_ref,
    kn_ref,
    vn_ref,
    resid_ref,
    wo_ref,
    ng_ref,
    wg_ref,
    wu_ref,
    wd_ref,
    out_ref,
    dec_ref,
    in_sem,
    s1_send,
    s1_recv,
    kv_send,
    kv_recv,
    x1_send,
    x1_recv,
    x2_send,
    x2_recv,
    xa_send,
    xa_recv,
    xb_send,
    xb_recv,
    xc_send,
    xc_recv,
    ring_send,
    ring_recv,
    out_sem,
):
    xlo, z, y = lax.axis_index("xlo"), lax.axis_index("z"), lax.axis_index("y")
    t = lax.axis_index("xhi") * 2 + lax.axis_index("core")
    p = xlo * NY + y

    def tp_dev(i):
        return {"xhi": i // 2, "core": i % 2}

    def plane_dev(i):
        return {"xlo": i // NY, "y": i % NY}

    def z_dev(i):
        return {"z": i % NZ}

    loads = {}
    for n, (name, src, dst) in enumerate(
        (
            ("wg", wg_hbm, wg_ref),
            ("wu", wu_hbm, wu_ref),
            ("wd", wd_hbm, wd_ref),
            ("k", k_hbm, k_ref),
            ("qg", qg_hbm, qg_ref),
            ("kg", kg_hbm, kg_ref),
            ("v", v_hbm, v_ref),
            ("qn", qn_hbm, qn_ref),
            ("kn", kn_hbm, kn_ref),
            ("vn", vn_hbm, vn_ref),
            ("gn", gn_hbm, gn_ref),
            ("resid", resid_hbm, resid_ref),
            ("gate", gate_hbm, gate_ref),
            ("wo", wo_hbm, wo_ref),
            ("ng", ng_hbm, ng_ref),
            ("q", q_hbm, q_ref),
        )
    ):
        loads[name] = pltpu.make_async_copy(src, dst, in_sem.at[n])
        loads[name].start()

    def arrive(*wanted):
        for name in wanted:
            loads[name].wait()

    barrier = pltpu.get_barrier_semaphore()
    mesh_id = pl.DeviceIdType.MESH
    for d in range(1, NT):
        pl.semaphore_signal(barrier, inc=1, device_id=tp_dev((t + d) % NT), device_id_type=mesh_id)
    for d in range(1, NP):
        pl.semaphore_signal(barrier, inc=1, device_id=plane_dev((p + d) % NP), device_id_type=mesh_id)
    for d in (1, 2, NZ - 2, NZ - 1):
        pl.semaphore_signal(barrier, inc=1, device_id=z_dev(z + d), device_id_type=mesh_id)

    started = []

    def send(src, dst, send_sem, recv_sem, device):
        copy = pltpu.make_async_remote_copy(
            src_ref=src,
            dst_ref=dst,
            send_sem=send_sem,
            recv_sem=recv_sem,
            device_id=device,
            device_id_type=mesh_id,
        )
        copy.start()
        started.append(copy)
        return copy

    arrive("wg", "wu", "wd")
    for n, ref in enumerate((wg_ref, wu_ref, wd_ref)):
        whole = ref[...].astype(f32)
        width = whole.shape[1]
        for i in range(NP):
            part = whole if i == 0 else roll(whole, width - CHUNK * i, 1)
            piece_out[i, :, n * 128 : (n + 1) * 128] = part[:, :128].astype(bf16)
    piece_in[pl.ds(p, 1)] = piece_out[pl.ds(p, 1)]

    pl.semaphore_wait(barrier, NT - 1 + NP - 1 + 4)
    s1 = [
        send(piece_out.at[(p + d) % NP], piece_in.at[p], s1_send.at[d - 1], s1_recv.at[d - 1], plane_dev((p + d) % NP))
        for d in range(1, NP)
    ]

    len0, len1, len2 = lengths_ref[0, 0], lengths_ref[0, 1], lengths_ref[0, 2]
    end0, end1 = len0, len0 + len1
    end2 = end1 + len2

    def start_of(index):
        return jnp.where(index >= end1, end1, jnp.where(index >= end0, end0, 0))

    own_index = t * TOK + iota((TOK, 128), 0)
    cosine, sine = rope_tables((own_index - start_of(own_index)).astype(f32))
    cos_t[...] = cosine
    sin_t[...] = sine

    arrive("k", "qg", "kg", "v")
    k_gain = kg_ref[...]
    q_gain = qg_ref[...]
    for k in range(KVH):
        lanes = slice(k * HD, (k + 1) * HD)
        keys[2, :, lanes] = norm_rope(k_ref[:, lanes].astype(f32), k_gain, cosine, sine).astype(bf16)
    for d in (1, 2):

        @pl.when(t + d < NT)
        def _(d=d):
            for n, (src, dst) in enumerate(((keys.at[2], keys.at[2 - d]), (v_ref, vals.at[2 - d]))):
                pltpu.make_async_remote_copy(
                    src_ref=src,
                    dst_ref=dst,
                    send_sem=kv_send.at[d - 1, n],
                    recv_sem=kv_recv.at[d - 1, n],
                    device_id=tp_dev(lax.rem(t + d, NT)),
                    device_id_type=mesh_id,
                ).start()

        @pl.when(t < d)
        def _(d=d):
            keys[2 - d] = jnp.zeros((TOK, KVH * HD), bf16)
            vals[2 - d] = jnp.zeros((TOK, KVH * HD), bf16)

    arrive("qn", "kn", "vn", "gn")
    for ref in (nq, nk, nv, ngate):
        ref[...] = jnp.zeros_like(ref)
    for h in range(HEADS):
        rows = slice(h * 4, h * 4 + 3)
        lanes = slice(h * HD, (h + 1) * HD)
        kv_lanes = slice(h // 2 * HD, (h // 2 + 1) * HD)
        nq[rows, :] = qn_ref[:, lanes].astype(f32)
        nk[rows, :] = kn_ref[:, kv_lanes].astype(f32)
        nv[rows, :] = vn_ref[:, kv_lanes].astype(f32)
        ngate[rows, :] = jnp.broadcast_to(gn_ref[:, h : h + 1].astype(f32), (3, HD))
    request = iota((HEADS * 4, HD), 0) % 4
    new_pos = jnp.where(request == 0, len0, jnp.where(request == 1, len1, jnp.where(request == 2, len2, 0)))
    new_cos, new_sin = rope_tables(new_pos.astype(f32))
    scale = HD**-0.5
    new_q = norm_rope(nq[...], q_gain, new_cos, new_sin).astype(bf16)
    new_k = norm_rope(nk[...], k_gain, new_cos, new_sin).astype(bf16)
    self_score = jnp.sum(new_q.astype(f32) * new_k.astype(f32), axis=-1, keepdims=True) * scale
    selfw[...] = jnp.broadcast_to(jnp.exp(self_score), selfw.shape)
    nq[...] = new_q.astype(f32)

    row_req = iota((8, TOK), 0) % 4
    token = t * TOK + iota((8, TOK), 1)
    begin = jnp.where(row_req == 0, 0, jnp.where(row_req == 1, end0, jnp.where(row_req == 2, end1, 0)))
    finish = jnp.where(row_req == 0, end0, jnp.where(row_req == 1, end1, jnp.where(row_req == 2, end2, 0)))
    own_bias = jnp.where((token >= begin) & (token < finish), 0.0, MASKED)
    for k in range(KVH):
        lanes = slice(k * HD, (k + 1) * HD)
        scores = nt_dot(nq[k * 8 : (k + 1) * 8, :].astype(bf16), keys[2, :, lanes]) * scale
        weights = jnp.exp(scores + own_bias)
        x1_out[k, 0:8, :] = jnp.dot(weights.astype(bf16), v_ref[:, lanes], preferred_element_type=f32)
        x1_out[k, 8:16, :] = jnp.broadcast_to(jnp.sum(weights, axis=-1, keepdims=True), (8, HD))
    x1_in[pl.ds(t, 1)] = x1_out[pl.ds(t, 1)]
    c1 = [
        send(x1_out.at[(t + d) % NT], x1_in.at[t], x1_send.at[d - 1], x1_recv.at[d - 1], tp_dev((t + d) % NT))
        for d in range(1, NT)
    ]

    for copy in s1:
        copy.wait_recv()
    block = piece_in[...].reshape(NP * 16, 3 * 128).astype(f32)
    for n in range(3):
        turned = jnp.transpose(block[:, n * 128 : (n + 1) * 128])
        gathered[pl.ds(z, 1), n * CHUNK : (n + 1) * CHUNK, :] = turned[:CHUNK, :].astype(bf16)[None]

    far = {}
    near = []

    def pass_on(step, chunk, backward):
        key = (step, chunk, backward)
        if step > 1:
            far[(step - 1, chunk, backward)].wait_recv()
        sign = NZ - 1 if backward else 1
        origin = (z + (NZ - sign) * 2 * (step - 1)) % NZ
        slot = gathered.at[origin, pl.ds(chunk * ROWS, ROWS)]
        for reach in (2, 1):
            if backward and step == 4 and reach == 2:
                continue
            n = (((step - 1) * CHUNKS + chunk) * 2 + int(backward)) * 2 + reach - 1
            copy = send(slot, slot, ring_send.at[n], ring_recv.at[n], z_dev(z + sign * reach))
            if reach == 2 and step < 4:
                far[key] = copy
            else:
                near.append(copy)

    def ring_step(step):
        for chunk in range(CHUNKS):
            for backward in (False, True):
                pass_on(step, chunk, backward)

    ring_step(1)

    arrive("resid", "gate")
    low = iota((8, 1024), 0) < 4
    fold[...] = jnp.zeros_like(fold)
    fold[0:3, :] = resid_ref[:, :1024].astype(f32)
    fold[4:7, :] = resid_ref[:, 1024:].astype(f32)
    key_index = (t - 2) * TOK + iota((TOK, 3 * TOK), 1)
    query_index = t * TOK + iota((TOK, 3 * TOK), 0)
    allowed = (key_index >= start_of(query_index)) & (key_index <= query_index)
    bias[...] = jnp.where(allowed, 0.0, MASKED)
    gate_rows = jax.nn.sigmoid(gate_ref[...].astype(f32))
    gates[...] = jnp.transpose(jnp.concatenate([gate_rows, jnp.zeros((120, TOK), f32)], axis=0))

    arrive("wo")
    for copy in c1:
        copy.wait_recv()
    both = x1_in[0] + x1_in[1] + x1_in[2] + x1_in[3]
    mine = pl.ds(pl.multiple_of(t * 8, 8), 8)
    own_self = selfw[mine, :]
    mixed = both[0:8] + own_self * nv[mine, :]
    attended = (mixed / (both[8:16] + own_self) * jax.nn.sigmoid(ngate[mine, :])).astype(bf16)
    first = jnp.dot(attended, wo_ref[0:HD, :], preferred_element_type=f32)
    second = jnp.dot(attended, wo_ref[HD : 2 * HD, :], preferred_element_type=f32)
    sums = first + roll(second, 4, 0)
    x2[pl.ds(t, 1)] = jnp.where(low, sums[:, :1024], roll(sums[:, 1024:], 4, 0)).astype(bf16)[None]
    c2 = [
        send(x2.at[t], x2.at[t], x2_send.at[d - 1], x2_recv.at[d - 1], tp_dev((t + d) % NT))
        for d in range(1, NT)
    ]
    for d in (1, 2):

        @pl.when(t >= d)
        def _(d=d):
            for n, (src, dst) in enumerate(((keys.at[2], keys.at[2 - d]), (v_ref, vals.at[2 - d]))):
                pltpu.make_async_remote_copy(
                    src_ref=src,
                    dst_ref=dst,
                    send_sem=kv_send.at[d - 1, n],
                    recv_sem=kv_recv.at[d - 1, n],
                    device_id=tp_dev(lax.rem(t + d, NT)),
                    device_id_type=mesh_id,
                ).wait_recv()

    arrive("q", "ng")
    def attend(h):
        lanes = slice(h * HD, (h + 1) * HD)
        kv_lanes = slice(h // 2 * HD, (h // 2 + 1) * HD)
        query = norm_rope(q_ref[:, lanes].astype(f32), q_gain, cos_t[...], sin_t[...]).astype(bf16)
        total = jnp.zeros((TOK, 1), f32)
        mixed = jnp.zeros((TOK, HD), f32)
        for b in range(3):
            scores = nt_dot(query, keys[b, :, kv_lanes]) * scale
            weights = jnp.exp(scores + bias[:, b * TOK : (b + 1) * TOK])
            total = total + jnp.sum(weights, axis=-1, keepdims=True)
            value = v_ref[:, kv_lanes] if b == 2 else vals[b, :, kv_lanes]
            mixed = mixed + jnp.dot(weights.astype(bf16), value, preferred_element_type=f32)
        out_ref[:, lanes] = (mixed / total * gates[:, h : h + 1]).astype(bf16)

    attend(0)
    ring_step(2)
    attend(1)

    for copy in c2:
        copy.wait_recv()
    attn = x2[0].astype(f32) + x2[1].astype(f32) + x2[2].astype(f32) + x2[3].astype(f32)
    hidden = fold[...] + attn
    squares = jnp.sum(hidden * hidden, axis=-1, keepdims=True)
    squares = jnp.broadcast_to(squares, (8, 128))
    mean_sq = ((squares + roll(squares, 4, 0)) / 2048.0)[:, 0:1]
    gain = jnp.where(low, ng_ref[:, :1024], ng_ref[:, 1024:])
    normed = hidden * lax.rsqrt(mean_sq + norm_eps) * gain
    xa[pl.ds(p, 1)] = swap_halves(normed).astype(bf16)[None]
    ca = [
        send(xa.at[p], xa.at[p], xa_send.at[d - 1], xa_recv.at[d - 1], plane_dev((p + d) % NP))
        for d in range(1, NP)
    ]
    attend(2)
    ring_step(3)
    attend(3)
    attend(4)
    ring_step(4)
    for h in range(5, HEADS):
        attend(h)
    result_copy = pltpu.make_async_copy(out_ref, out_hbm, out_sem.at[0])
    result_copy.start()
    for copy in near:
        copy.wait_recv()

    for copy in ca:
        copy.wait_recv()
    tokens = xa[...].astype(f32).reshape(NP * 8, 1024).astype(bf16)
    parts = []
    for n in range(2):
        halves = []
        for h in range(2):
            total = jnp.zeros((NP * 8, CHUNK), f32)
            for j in range(NZ // 2):
                total = total + nt_dot(
                    tokens[:, j * 128 : (j + 1) * 128],
                    gathered[2 * j + h, n * CHUNK : (n + 1) * CHUNK, :],
                )
            halves.append(total)
        parts.append(halves)
    shift = NP * 8 - 4
    unit_gate = parts[0][0] + roll(jnp.concatenate([parts[0][1], jnp.zeros((NP * 8, 32), f32)], axis=1), shift, 0)[:, :CHUNK]
    unit_up = parts[1][0] + roll(jnp.concatenate([parts[1][1], jnp.zeros((NP * 8, 32), f32)], axis=1), shift, 0)[:, :CHUNK]
    units = (unit_gate / (1.0 + jnp.exp(-unit_gate)) * unit_up).astype(bf16)
    low_rows = iota((NP * 8, 128), 0) % 8 < 4
    for j in range(NZ // 2):
        even = jnp.dot(units, gathered[2 * j, 2 * CHUNK : 3 * CHUNK, :], preferred_element_type=f32)
        odd = jnp.dot(units, gathered[2 * j + 1, 2 * CHUNK : 3 * CHUNK, :], preferred_element_type=f32)
        xb_out[:, :, j * 128 : (j + 1) * 128] = jnp.where(low_rows, even, roll(odd, 4, 0)).reshape(NP, 8, 128).astype(bf16)
    xb_in[pl.ds(p, 1)] = xb_out[pl.ds(p, 1)]
    cb = [
        send(xb_out.at[(p + d) % NP], xb_in.at[p], xb_send.at[d - 1], xb_recv.at[d - 1], plane_dev((p + d) % NP))
        for d in range(1, NP)
    ]
    for copy in cb:
        copy.wait_recv()
    total = xb_in[0].astype(f32)
    for i in range(1, NP):
        total = total + xb_in[i].astype(f32)
    xc[pl.ds(t, 1)] = total.astype(bf16)[None]
    cc = [
        send(xc.at[t], xc.at[t], xc_send.at[d - 1], xc_recv.at[d - 1], tp_dev((t + d) % NT))
        for d in range(1, NT)
    ]
    for copy in cc:
        copy.wait_recv()
    down = xc[0].astype(f32) + xc[1].astype(f32) + xc[2].astype(f32) + xc[3].astype(f32)
    result = (hidden + swap_halves(down)).astype(bf16)
    dec_ref[:, :1024] = result[0:3]
    dec_ref[:, 1024:] = result[4:7]
    last_copy = pltpu.make_async_copy(dec_ref, dec_hbm, out_sem.at[1])
    last_copy.start()

    for copy in started:
        copy.wait_send()
    result_copy.wait()
    last_copy.wait()
    for d in (1, 2):

        @pl.when(t + d < NT)
        def _(d=d):
            for n, (src, dst) in enumerate(((keys.at[2], keys.at[2 - d]), (v_ref, vals.at[2 - d]))):
                pltpu.make_async_remote_copy(
                    src_ref=src,
                    dst_ref=dst,
                    send_sem=kv_send.at[d - 1, n],
                    recv_sem=kv_recv.at[d - 1, n],
                    device_id=tp_dev(lax.rem(t + d, NT)),
                    device_id_type=mesh_id,
                ).wait_send()


def local(
    q_pre,
    gate_pre,
    k_pre,
    v_pre,
    q_gain,
    k_gain,
    lengths,
    q_new,
    gate_new,
    k_new,
    v_new,
    resid,
    w_out,
    norm_gain,
    w_gate,
    w_up,
    w_down,
):
    dma = pltpu.SemaphoreType.DMA
    return pl.pallas_call(
        kernel,
        out_shape=(
            jax.ShapeDtypeStruct((TOK, HEADS * HD), bf16),
            jax.ShapeDtypeStruct((3, 2048), bf16),
        ),
        in_specs=[pl.BlockSpec(memory_space=pltpu.SMEM)] + [pl.BlockSpec(memory_space=pltpu.HBM)] * 16,
        out_specs=(pl.BlockSpec(memory_space=pltpu.HBM),) * 2,
        scratch_shapes=[
            pltpu.VMEM((3, TOK, KVH * HD), bf16),
            pltpu.VMEM((2, TOK, KVH * HD), bf16),
            pltpu.VMEM((TOK, 3 * TOK), f32),
            pltpu.VMEM((HEADS * 4, HD), f32),
            pltpu.VMEM((HEADS * 4, HD), f32),
            pltpu.VMEM((HEADS * 4, HD), f32),
            pltpu.VMEM((HEADS * 4, HD), f32),
            pltpu.VMEM((HEADS * 4, HD), f32),
            pltpu.VMEM((8, 1024), f32),
            pltpu.VMEM((NP, 16, 384), bf16),
            pltpu.VMEM((NP, 16, 384), bf16),
            pltpu.VMEM((NZ, 3 * CHUNK, 128), bf16),
            pltpu.VMEM((NT, 16, 128), f32),
            pltpu.VMEM((NT, 16, 128), f32),
            pltpu.VMEM((NT, 8, 1024), bf16),
            pltpu.VMEM((NP, 8, 1024), bf16),
            pltpu.VMEM((NP, 8, 1024), bf16),
            pltpu.VMEM((NP, 8, 1024), bf16),
            pltpu.VMEM((NT, 8, 1024), bf16),
            pltpu.VMEM((TOK, HD), f32),
            pltpu.VMEM((TOK, HD), f32),
            pltpu.VMEM((TOK, 128), f32),
            pltpu.VMEM((TOK, HEADS * HD), bf16),
            pltpu.VMEM((HEADS, TOK), bf16),
            pltpu.VMEM((TOK, KVH * HD), bf16),
            pltpu.VMEM((TOK, KVH * HD), bf16),
            pltpu.VMEM((1, HD), f32),
            pltpu.VMEM((1, HD), f32),
            pltpu.VMEM((3, HEADS * HD), bf16),
            pltpu.VMEM((3, HEADS), bf16),
            pltpu.VMEM((3, KVH * HD), bf16),
            pltpu.VMEM((3, KVH * HD), bf16),
            pltpu.VMEM((3, 2048), bf16),
            pltpu.VMEM((2 * HD, 2048), bf16),
            pltpu.VMEM((1, 2048), f32),
            pltpu.VMEM((16, 768), bf16),
            pltpu.VMEM((16, 768), bf16),
            pltpu.VMEM((16, 768), bf16),
            pltpu.VMEM((TOK, HEADS * HD), bf16),
            pltpu.VMEM((3, 2048), bf16),
            dma((16,)),
            dma((NP - 1,)),
            dma((NP - 1,)),
            dma((2, 2)),
            dma((2, 2)),
            dma((NT - 1,)),
            dma((NT - 1,)),
            dma((NT - 1,)),
            dma((NT - 1,)),
            dma((NP - 1,)),
            dma((NP - 1,)),
            dma((NP - 1,)),
            dma((NP - 1,)),
            dma((NT - 1,)),
            dma((NT - 1,)),
            dma((4 * CHUNKS * 4,)),
            dma((4 * CHUNKS * 4,)),
            dma((2,)),
        ],
        compiler_params=pltpu.CompilerParams(
            collective_id=0, has_side_effects=True, vmem_limit_bytes=60 * 1024 * 1024
        ),
    )(
        lengths,
        q_pre,
        gate_pre.T,
        k_pre,
        v_pre,
        q_gain.reshape(1, HD),
        k_gain.reshape(1, HD),
        q_new,
        gate_new,
        k_new,
        v_new,
        resid,
        w_out,
        norm_gain.reshape(1, 2048),
        w_gate,
        w_up,
        w_down.T,
    )


def solution(mesh):
    wide = jax.sharding.Mesh(
        mesh.devices.reshape(NX, NZ, NY, 2, 2), ("xlo", "z", "y", "xhi", "core")
    )
    return jax.shard_map(
        local,
        mesh=wide,
        in_specs=(
            P(req + tp, None),
            P(req + tp, None),
            P(req + tp, None),
            P(req + tp, None),
            P(),
            P(),
            P(req, None),
            P(req, None),
            P(req, None),
            P(req, None),
            P(req, None),
            P(req, None),
            P(tp, None),
            P(),
            P(req, tp),
            P(req, tp),
            P(tp, req),
        ),
        out_specs=(P(req + tp, None), P(req, None)),
        check_vma=False,
    )
```

```python
import functools

import jax
import jax.numpy as jnp
from jax import lax
from jax.experimental import pallas as pl
from jax.experimental.pallas import tpu as pltpu
from jax.sharding import PartitionSpec as P

rope_base = 1000000.0
norm_eps = 1e-06
req = ("xlo", "z", "y")
tp = ("xhi", "core")
NX, NZ, NY, NT = 2, 16, 4, 4
NP = NX * NY
HD = 128
HEADS = 8
KVH = 4
TOK = 128
CHUNK = 96
CHUNKS = 2
ROWS = 3 * CHUNK // CHUNKS
MASKED = -1e30
f32 = jnp.float32
bf16 = jnp.bfloat16


def iota(shape, dim):
    return lax.broadcasted_iota(jnp.int32, shape, dim)


def roll(values, shift, axis):
    return pltpu.roll(values, shift, axis)


def nt_dot(a, b):
    return lax.dot_general(a, b, (((1,), (1,)), ((), ())), preferred_element_type=f32)


def angle_tables(position):
    lane = iota(position.shape, 1)
    index = (lane % 64).astype(f32)
    freqs = jnp.exp(index * (-2.0 / HD * 13.815510557964274))
    angles = position * freqs
    return jnp.cos(angles), jnp.sin(angles)


def norm_rope(values, gain, cosine, sine):
    mean_sq = jnp.mean(values * values, axis=-1, keepdims=True)
    normed = values * lax.rsqrt(mean_sq + norm_eps) * gain
    return normed * cosine + roll(normed, 64, 1) * sine


def swap_halves(values):
    keep = (iota((8, 128), 0) < 4) == (iota((8, 128), 1) < 64)
    tiles = []
    for j in range(values.shape[1] // 128):
        tile = values[:, j * 128 : (j + 1) * 128]
        tiles.append(jnp.where(keep, tile, roll(roll(tile, 64, 1), 4, 0)))
    return jnp.concatenate(tiles, axis=1)


def kernel(
    lengths_ref,
    q_hbm,
    gate_hbm,
    k_hbm,
    v_hbm,
    qg_hbm,
    kg_hbm,
    qn_hbm,
    gn_hbm,
    kn_hbm,
    vn_hbm,
    resid_hbm,
    wo_hbm,
    ng_hbm,
    wg_hbm,
    wu_hbm,
    wd_hbm,
    out_hbm,
    dec_hbm,
    keys,
    vals,
    bias,
    nq,
    nk,
    nv,
    ngate,
    selfw,
    fold,
    piece_out,
    piece_in,
    gathered,
    x1_out,
    x1_in,
    x2,
    xa,
    xb_out,
    xb_in,
    xc,
    cos_t,
    sin_t,
    gates,
    q_ref,
    gate_ref,
    k_ref,
    v_ref,
    qg_ref,
    kg_ref,
    qn_ref,
    gn_ref,
    kn_ref,
    vn_ref,
    resid_ref,
    wo_ref,
    ng_ref,
    wg_ref,
    wu_ref,
    wd_ref,
    out_ref,
    dec_ref,
    in_sem,
    s1_send,
    s1_recv,
    kv_send,
    kv_recv,
    x1_send,
    x1_recv,
    x2_send,
    x2_recv,
    xa_send,
    xa_recv,
    xb_send,
    xb_recv,
    xc_send,
    xc_recv,
    ring_send,
    ring_recv,
    out_sem,
):
    xlo, z, y = lax.axis_index("xlo"), lax.axis_index("z"), lax.axis_index("y")
    t = lax.axis_index("xhi") * 2 + lax.axis_index("core")
    p = xlo * NY + y

    def tp_dev(i):
        return {"xhi": i // 2, "core": i % 2}

    def plane_dev(i):
        return {"xlo": i // NY, "y": i % NY}

    def z_dev(i):
        return {"z": i % NZ}

    loads = {}
    for n, (name, src, dst) in enumerate(
        (
            ("wg", wg_hbm, wg_ref),
            ("wu", wu_hbm, wu_ref),
            ("wd", wd_hbm, wd_ref),
            ("k", k_hbm, k_ref),
            ("qg", qg_hbm, qg_ref),
            ("kg", kg_hbm, kg_ref),
            ("v", v_hbm, v_ref),
            ("qn", qn_hbm, qn_ref),
            ("kn", kn_hbm, kn_ref),
            ("vn", vn_hbm, vn_ref),
            ("gn", gn_hbm, gn_ref),
            ("resid", resid_hbm, resid_ref),
            ("gate", gate_hbm, gate_ref),
            ("wo", wo_hbm, wo_ref),
            ("ng", ng_hbm, ng_ref),
            ("q", q_hbm, q_ref),
        )
    ):
        loads[name] = pltpu.make_async_copy(src, dst, in_sem.at[n])
        loads[name].start()

    def arrive(*wanted):
        for name in wanted:
            loads[name].wait()

    barrier = pltpu.get_barrier_semaphore()
    mesh_id = pl.DeviceIdType.MESH
    for d in range(1, NT):
        pl.semaphore_signal(barrier, inc=1, device_id=tp_dev((t + d) % NT), device_id_type=mesh_id)
    for d in range(1, NP):
        pl.semaphore_signal(barrier, inc=1, device_id=plane_dev((p + d) % NP), device_id_type=mesh_id)
    for d in (1, 2, NZ - 2, NZ - 1):
        pl.semaphore_signal(barrier, inc=1, device_id=z_dev(z + d), device_id_type=mesh_id)

    started = []

    def send(src, dst, send_sem, recv_sem, device):
        copy = pltpu.make_async_remote_copy(
            src_ref=src,
            dst_ref=dst,
            send_sem=send_sem,
            recv_sem=recv_sem,
            device_id=device,
            device_id_type=mesh_id,
        )
        copy.start()
        started.append(copy)
        return copy

    arrive("wg", "wu", "wd")
    for n, ref in enumerate((wg_ref, wu_ref, wd_ref)):
        whole = ref[...].astype(f32)
        width = whole.shape[1]
        for i in range(NP):
            part = whole if i == 0 else roll(whole, width - CHUNK * i, 1)
            piece_out[i, :, n * 128 : (n + 1) * 128] = part[:, :128].astype(bf16)
    piece_in[pl.ds(p, 1)] = piece_out[pl.ds(p, 1)]

    len0, len1, len2 = lengths_ref[0, 0], lengths_ref[0, 1], lengths_ref[0, 2]
    end0, end1 = len0, len0 + len1
    end2 = end1 + len2

    def start_of(index):
        return jnp.where(index >= end1, end1, jnp.where(index >= end0, end0, 0))

    left = iota((TOK // 2, 128), 1) < 64
    own_index = t * TOK + iota((TOK // 2, 128), 0) + jnp.where(left, 0, TOK // 2)
    for ref, packed, sign in zip((cos_t, sin_t), angle_tables((own_index - start_of(own_index)).astype(f32)), (1.0, -1.0)):
        turned = roll(packed, 64, 1)
        ref[: TOK // 2, :] = jnp.where(left, sign * packed, turned)
        ref[TOK // 2 :, :] = jnp.where(left, sign * turned, packed)
    cosine, sine = cos_t[...], sin_t[...]

    arrive("k", "qg", "kg", "v")
    k_gain = kg_ref[...]
    q_gain = qg_ref[...]
    for k in range(KVH):
        lanes = slice(k * HD, (k + 1) * HD)
        keys[2, :, lanes] = norm_rope(k_ref[:, lanes].astype(f32), k_gain, cosine, sine).astype(bf16)
    arrive("qn", "kn", "vn", "gn")
    for ref in (nq, nk, nv, ngate):
        ref[...] = jnp.zeros_like(ref)
    for h in range(HEADS):
        rows = slice(h * 4, h * 4 + 3)
        lanes = slice(h * HD, (h + 1) * HD)
        kv_lanes = slice(h // 2 * HD, (h // 2 + 1) * HD)
        nq[rows, :] = qn_ref[:, lanes].astype(f32)
        nk[rows, :] = kn_ref[:, kv_lanes].astype(f32)
        nv[rows, :] = vn_ref[:, kv_lanes].astype(f32)
        ngate[rows, :] = jnp.broadcast_to(gn_ref[:, h : h + 1].astype(f32), (3, HD))
    request = iota((8, HD), 0) % 4
    new_pos = jnp.where(request == 0, len0, jnp.where(request == 1, len1, jnp.where(request == 2, len2, 0)))
    new_cos, new_sin = angle_tables(new_pos.astype(f32))
    new_sin = jnp.where(iota((8, HD), 1) < 64, -new_sin, new_sin)
    new_cos = jnp.concatenate([new_cos] * 4, axis=0)
    new_sin = jnp.concatenate([new_sin] * 4, axis=0)
    scale = HD**-0.5
    new_q = norm_rope(nq[...], q_gain, new_cos, new_sin).astype(bf16)
    new_k = norm_rope(nk[...], k_gain, new_cos, new_sin).astype(bf16)
    self_score = jnp.sum(new_q.astype(f32) * new_k.astype(f32), axis=-1, keepdims=True) * scale
    selfw[...] = jnp.broadcast_to(jnp.exp(self_score), selfw.shape)
    nq[...] = new_q.astype(f32)

    row_req = iota((8, TOK), 0) % 4
    token = t * TOK + iota((8, TOK), 1)
    begin = jnp.where(row_req == 0, 0, jnp.where(row_req == 1, end0, jnp.where(row_req == 2, end1, 0)))
    finish = jnp.where(row_req == 0, end0, jnp.where(row_req == 1, end1, jnp.where(row_req == 2, end2, 0)))
    own_bias = jnp.where((token >= begin) & (token < finish), 0.0, MASKED)
    for k in range(KVH):
        lanes = slice(k * HD, (k + 1) * HD)
        scores = nt_dot(nq[k * 8 : (k + 1) * 8, :].astype(bf16), keys[2, :, lanes]) * scale
        weights = jnp.exp(scores + own_bias)
        x1_out[k, 0:8, :] = jnp.dot(weights.astype(bf16), v_ref[:, lanes], preferred_element_type=f32)
        x1_out[k, 8:16, :] = jnp.broadcast_to(jnp.sum(weights, axis=-1, keepdims=True), (8, HD))
    x1_in[pl.ds(t, 1)] = x1_out[pl.ds(t, 1)]
    pl.semaphore_wait(barrier, NT - 1 + NP - 1 + 4)
    s1 = [
        send(piece_out.at[(p + d) % NP], piece_in.at[p], s1_send.at[d - 1], s1_recv.at[d - 1], plane_dev((p + d) % NP))
        for d in range(1, NP)
    ]

    c1 = [
        send(x1_out.at[(t + d) % NT], x1_in.at[t], x1_send.at[d - 1], x1_recv.at[d - 1], tp_dev((t + d) % NT))
        for d in range(1, NT)
    ]
    for d in (1, 2):

        @pl.when(t + d < NT)
        def _(d=d):
            for n, (src, dst) in enumerate(((keys.at[2], keys.at[2 - d]), (v_ref, vals.at[2 - d]))):
                pltpu.make_async_remote_copy(
                    src_ref=src,
                    dst_ref=dst,
                    send_sem=kv_send.at[d - 1, n],
                    recv_sem=kv_recv.at[d - 1, n],
                    device_id=tp_dev(lax.rem(t + d, NT)),
                    device_id_type=mesh_id,
                ).start()

        @pl.when(t < d)
        def _(d=d):
            keys[2 - d] = jnp.zeros((TOK, KVH * HD), bf16)
            vals[2 - d] = jnp.zeros((TOK, KVH * HD), bf16)


    for copy in s1:
        copy.wait_recv()
    block = piece_in[...].reshape(NP * 16, 3 * 128).astype(f32)
    for n in range(3):
        turned = jnp.transpose(block[:, n * 128 : (n + 1) * 128])
        gathered[pl.ds(z, 1), n * CHUNK : (n + 1) * CHUNK, :] = turned[:CHUNK, :].astype(bf16)[None]

    far = {}
    near = []

    def pass_on(step, chunk, backward):
        key = (step, chunk, backward)
        if step > 1:
            far[(step - 1, chunk, backward)].wait_recv()
        sign = NZ - 1 if backward else 1
        origin = (z + (NZ - sign) * 2 * (step - 1)) % NZ
        slot = gathered.at[origin, pl.ds(chunk * ROWS, ROWS)]
        for reach in (2, 1):
            if backward and step == 4 and reach == 2:
                continue
            n = (((step - 1) * CHUNKS + chunk) * 2 + int(backward)) * 2 + reach - 1
            copy = send(slot, slot, ring_send.at[n], ring_recv.at[n], z_dev(z + sign * reach))
            if reach == 2 and step < 4:
                far[key] = copy
            else:
                near.append((step, copy))

    def ring_step(step):
        for chunk in range(CHUNKS):
            for backward in (False, True):
                pass_on(step, chunk, backward)

    ring_step(1)

    arrive("resid", "gate")
    low = iota((8, 1024), 0) < 4
    fold[...] = jnp.zeros_like(fold)
    fold[0:3, :] = resid_ref[:, :1024].astype(f32)
    fold[4:7, :] = resid_ref[:, 1024:].astype(f32)
    key_index = (t - 2) * TOK + iota((TOK, 3 * TOK), 1)
    query_index = t * TOK + iota((TOK, 3 * TOK), 0)
    allowed = (key_index >= start_of(query_index)) & (key_index <= query_index)
    bias[...] = jnp.where(allowed, 0.0, MASKED)
    gate_rows = jax.nn.sigmoid(gate_ref[...].astype(f32))
    gates[...] = jnp.transpose(jnp.concatenate([gate_rows, jnp.zeros((120, TOK), f32)], axis=0))

    arrive("wo")
    for copy in c1:
        copy.wait_recv()
    both = x1_in[0] + x1_in[1] + x1_in[2] + x1_in[3]
    mine = pl.ds(pl.multiple_of(t * 8, 8), 8)
    own_self = selfw[mine, :]
    mixed = both[0:8] + own_self * nv[mine, :]
    attended = (mixed / (both[8:16] + own_self) * jax.nn.sigmoid(ngate[mine, :])).astype(bf16)
    first = jnp.dot(attended, wo_ref[0:HD, :], preferred_element_type=f32)
    second = jnp.dot(attended, wo_ref[HD : 2 * HD, :], preferred_element_type=f32)
    sums = first + roll(second, 4, 0)
    x2[pl.ds(t, 1)] = jnp.where(low, sums[:, :1024], roll(sums[:, 1024:], 4, 0)).astype(bf16)[None]
    c2 = [
        send(x2.at[t], x2.at[t], x2_send.at[d - 1], x2_recv.at[d - 1], tp_dev((t + d) % NT))
        for d in range(1, NT)
    ]
    for d in (1, 2):

        @pl.when(t >= d)
        def _(d=d):
            for n, (src, dst) in enumerate(((keys.at[2], keys.at[2 - d]), (v_ref, vals.at[2 - d]))):
                pltpu.make_async_remote_copy(
                    src_ref=src,
                    dst_ref=dst,
                    send_sem=kv_send.at[d - 1, n],
                    recv_sem=kv_recv.at[d - 1, n],
                    device_id=tp_dev(lax.rem(t + d, NT)),
                    device_id_type=mesh_id,
                ).wait_recv()

    arrive("q", "ng")
    def attend(h):
        lanes = slice(h * HD, (h + 1) * HD)
        kv_lanes = slice(h // 2 * HD, (h // 2 + 1) * HD)
        query = norm_rope(q_ref[:, lanes].astype(f32), q_gain, cos_t[...], sin_t[...]).astype(bf16)
        total = jnp.zeros((TOK, 1), f32)
        mixed = jnp.zeros((TOK, HD), f32)
        for b in range(3):
            scores = nt_dot(query, keys[b, :, kv_lanes]) * scale
            weights = jnp.exp(scores + bias[:, b * TOK : (b + 1) * TOK])
            total = total + jnp.sum(weights, axis=-1, keepdims=True)
            value = v_ref[:, kv_lanes] if b == 2 else vals[b, :, kv_lanes]
            mixed = mixed + jnp.dot(weights.astype(bf16), value, preferred_element_type=f32)
        out_ref[:, lanes] = (mixed / total * gates[:, h : h + 1]).astype(bf16)

    ring_step(2)
    attend(0)
    attend(1)

    for copy in c2:
        copy.wait_recv()
    attn = x2[0].astype(f32) + x2[1].astype(f32) + x2[2].astype(f32) + x2[3].astype(f32)
    hidden = fold[...] + attn
    squares = jnp.sum(hidden * hidden, axis=-1, keepdims=True)
    squares = jnp.broadcast_to(squares, (8, 128))
    mean_sq = ((squares + roll(squares, 4, 0)) / 2048.0)[:, 0:1]
    gain = jnp.where(low, ng_ref[:, :1024], ng_ref[:, 1024:])
    normed = hidden * lax.rsqrt(mean_sq + norm_eps) * gain
    xa[pl.ds(p, 1)] = swap_halves(normed).astype(bf16)[None]
    ca = [
        send(xa.at[p], xa.at[p], xa_send.at[d - 1], xa_recv.at[d - 1], plane_dev((p + d) % NP))
        for d in range(1, NP)
    ]
    ring_step(3)
    attend(2)
    attend(3)
    attend(4)
    ring_step(4)
    for h in range(5, HEADS):
        attend(h)
    result_copy = pltpu.make_async_copy(out_ref, out_hbm, out_sem.at[0])
    result_copy.start()

    for copy in ca:
        copy.wait_recv()

    def product(away):
        origin = (z + NZ + away) % NZ
        lanes = pl.ds(pl.multiple_of(origin // 2 * 128, 128), 128)
        tokens = xa[:, :, lanes].astype(f32).reshape(NP * 8, 128).astype(bf16)
        return nt_dot(tokens, gathered[pl.ds(origin, 1), 0 : 2 * CHUNK, :][0])

    same = product(0)
    for away in (2, -2, 4, -4):
        same = same + product(away)
    for step, copy in near:
        if step < 4:
            copy.wait_recv()
    other = product(1)
    for away in (-1, 3, -3, 5, -5):
        other = other + product(away)
    same = same + product(6) + product(-6)
    for step, copy in near:
        if step == 4:
            copy.wait_recv()
    same = same + product(8)
    other = other + product(7) + product(-7)
    fill = jnp.zeros((NP * 8, 256 - 2 * CHUNK), f32)
    same = jnp.concatenate([same, fill], axis=1)
    other = jnp.concatenate([other, fill], axis=1)
    swap = (iota((NP * 8, 256), 0) * 0 + z % 2) == 1
    sums = jnp.where(swap, other, same) + roll(jnp.where(swap, same, other), NP * 8 - 4, 0)
    unit_gate = sums[:, :CHUNK]
    unit_up = roll(sums, 256 - CHUNK, 1)[:, :CHUNK]
    units = (unit_gate / (1.0 + jnp.exp(-unit_gate)) * unit_up).astype(bf16)
    low_rows = iota((NP * 8, 128), 0) % 8 < 4
    for j in range(NZ // 2):
        even = jnp.dot(units, gathered[2 * j, 2 * CHUNK : 3 * CHUNK, :], preferred_element_type=f32)
        odd = jnp.dot(units, gathered[2 * j + 1, 2 * CHUNK : 3 * CHUNK, :], preferred_element_type=f32)
        xb_out[:, :, j * 128 : (j + 1) * 128] = jnp.where(low_rows, even, roll(odd, 4, 0)).reshape(NP, 8, 128).astype(bf16)
    xb_in[pl.ds(p, 1)] = xb_out[pl.ds(p, 1)]
    cb = [
        send(xb_out.at[(p + d) % NP], xb_in.at[p], xb_send.at[d - 1], xb_recv.at[d - 1], plane_dev((p + d) % NP))
        for d in range(1, NP)
    ]
    for copy in cb:
        copy.wait_recv()
    total = xb_in[0].astype(f32)
    for i in range(1, NP):
        total = total + xb_in[i].astype(f32)
    xc[pl.ds(t, 1)] = total.astype(bf16)[None]
    cc = [
        send(xc.at[t], xc.at[t], xc_send.at[d - 1], xc_recv.at[d - 1], tp_dev((t + d) % NT))
        for d in range(1, NT)
    ]
    for copy in cc:
        copy.wait_recv()
    down = xc[0].astype(f32) + xc[1].astype(f32) + xc[2].astype(f32) + xc[3].astype(f32)
    result = (hidden + swap_halves(down)).astype(bf16)
    dec_ref[:, :1024] = result[0:3]
    dec_ref[:, 1024:] = result[4:7]
    last_copy = pltpu.make_async_copy(dec_ref, dec_hbm, out_sem.at[1])
    last_copy.start()

    for copy in started:
        copy.wait_send()
    result_copy.wait()
    last_copy.wait()
    for d in (1, 2):

        @pl.when(t + d < NT)
        def _(d=d):
            for n, (src, dst) in enumerate(((keys.at[2], keys.at[2 - d]), (v_ref, vals.at[2 - d]))):
                pltpu.make_async_remote_copy(
                    src_ref=src,
                    dst_ref=dst,
                    send_sem=kv_send.at[d - 1, n],
                    recv_sem=kv_recv.at[d - 1, n],
                    device_id=tp_dev(lax.rem(t + d, NT)),
                    device_id_type=mesh_id,
                ).wait_send()


def local(
    q_pre,
    gate_pre,
    k_pre,
    v_pre,
    q_gain,
    k_gain,
    lengths,
    q_new,
    gate_new,
    k_new,
    v_new,
    resid,
    w_out,
    norm_gain,
    w_gate,
    w_up,
    w_down,
):
    dma = pltpu.SemaphoreType.DMA
    return pl.pallas_call(
        kernel,
        out_shape=(
            jax.ShapeDtypeStruct((TOK, HEADS * HD), bf16),
            jax.ShapeDtypeStruct((3, 2048), bf16),
        ),
        in_specs=[pl.BlockSpec(memory_space=pltpu.SMEM)] + [pl.BlockSpec(memory_space=pltpu.HBM)] * 16,
        out_specs=(pl.BlockSpec(memory_space=pltpu.HBM),) * 2,
        scratch_shapes=[
            pltpu.VMEM((3, TOK, KVH * HD), bf16),
            pltpu.VMEM((2, TOK, KVH * HD), bf16),
            pltpu.VMEM((TOK, 3 * TOK), f32),
            pltpu.VMEM((HEADS * 4, HD), f32),
            pltpu.VMEM((HEADS * 4, HD), f32),
            pltpu.VMEM((HEADS * 4, HD), f32),
            pltpu.VMEM((HEADS * 4, HD), f32),
            pltpu.VMEM((HEADS * 4, HD), f32),
            pltpu.VMEM((8, 1024), f32),
            pltpu.VMEM((NP, 16, 384), bf16),
            pltpu.VMEM((NP, 16, 384), bf16),
            pltpu.VMEM((NZ, 3 * CHUNK, 128), bf16),
            pltpu.VMEM((NT, 16, 128), f32),
            pltpu.VMEM((NT, 16, 128), f32),
            pltpu.VMEM((NT, 8, 1024), bf16),
            pltpu.VMEM((NP, 8, 1024), bf16),
            pltpu.VMEM((NP, 8, 1024), bf16),
            pltpu.VMEM((NP, 8, 1024), bf16),
            pltpu.VMEM((NT, 8, 1024), bf16),
            pltpu.VMEM((TOK, HD), f32),
            pltpu.VMEM((TOK, HD), f32),
            pltpu.VMEM((TOK, 128), f32),
            pltpu.VMEM((TOK, HEADS * HD), bf16),
            pltpu.VMEM((HEADS, TOK), bf16),
            pltpu.VMEM((TOK, KVH * HD), bf16),
            pltpu.VMEM((TOK, KVH * HD), bf16),
            pltpu.VMEM((1, HD), f32),
            pltpu.VMEM((1, HD), f32),
            pltpu.VMEM((3, HEADS * HD), bf16),
            pltpu.VMEM((3, HEADS), bf16),
            pltpu.VMEM((3, KVH * HD), bf16),
            pltpu.VMEM((3, KVH * HD), bf16),
            pltpu.VMEM((3, 2048), bf16),
            pltpu.VMEM((2 * HD, 2048), bf16),
            pltpu.VMEM((1, 2048), f32),
            pltpu.VMEM((16, 768), bf16),
            pltpu.VMEM((16, 768), bf16),
            pltpu.VMEM((16, 768), bf16),
            pltpu.VMEM((TOK, HEADS * HD), bf16),
            pltpu.VMEM((3, 2048), bf16),
            dma((16,)),
            dma((NP - 1,)),
            dma((NP - 1,)),
            dma((2, 2)),
            dma((2, 2)),
            dma((NT - 1,)),
            dma((NT - 1,)),
            dma((NT - 1,)),
            dma((NT - 1,)),
            dma((NP - 1,)),
            dma((NP - 1,)),
            dma((NP - 1,)),
            dma((NP - 1,)),
            dma((NT - 1,)),
            dma((NT - 1,)),
            dma((4 * CHUNKS * 4,)),
            dma((4 * CHUNKS * 4,)),
            dma((2,)),
        ],
        compiler_params=pltpu.CompilerParams(
            collective_id=0, has_side_effects=True, vmem_limit_bytes=60 * 1024 * 1024
        ),
    )(
        lengths,
        q_pre,
        gate_pre.T,
        k_pre,
        v_pre,
        q_gain.reshape(1, HD),
        k_gain.reshape(1, HD),
        q_new,
        gate_new,
        k_new,
        v_new,
        resid,
        w_out,
        norm_gain.reshape(1, 2048),
        w_gate,
        w_up,
        w_down.T,
    )


def solution(mesh):
    wide = jax.sharding.Mesh(
        mesh.devices.reshape(NX, NZ, NY, 2, 2), ("xlo", "z", "y", "xhi", "core")
    )
    return jax.shard_map(
        local,
        mesh=wide,
        in_specs=(
            P(req + tp, None),
            P(req + tp, None),
            P(req + tp, None),
            P(req + tp, None),
            P(),
            P(),
            P(req, None),
            P(req, None),
            P(req, None),
            P(req, None),
            P(req, None),
            P(req, None),
            P(tp, None),
            P(),
            P(req, tp),
            P(req, tp),
            P(tp, req),
        ),
        out_specs=(P(req + tp, None), P(req, None)),
        check_vma=False,
    )
```

```python
import functools

import jax
import jax.numpy as jnp
from jax import lax
from jax.experimental import pallas as pl
from jax.experimental.pallas import tpu as pltpu
from jax.sharding import PartitionSpec as P

rope_base = 1000000.0
norm_eps = 1e-06
req = ("xlo", "z", "y")
tp = ("xhi", "core")
NX, NZ, NY, NT = 2, 16, 4, 4
NP = NX * NY
HD = 128
HEADS = 8
KVH = 4
TOK = 128
CHUNK = 96
CHUNKS = 2
ROWS = 3 * CHUNK // CHUNKS
MASKED = -1e30
f32 = jnp.float32
bf16 = jnp.bfloat16


def iota(shape, dim):
    return lax.broadcasted_iota(jnp.int32, shape, dim)


def roll(values, shift, axis):
    return pltpu.roll(values, shift, axis)


def nt_dot(a, b):
    return lax.dot_general(a, b, (((1,), (1,)), ((), ())), preferred_element_type=f32)


def angle_tables(position):
    lane = iota(position.shape, 1)
    index = (lane % 64).astype(f32)
    freqs = jnp.exp(index * (-2.0 / HD * 13.815510557964274))
    angles = position * freqs
    return jnp.cos(angles), jnp.sin(angles)


def norm_rope(values, gain, cosine, sine):
    mean_sq = jnp.mean(values * values, axis=-1, keepdims=True)
    normed = values * lax.rsqrt(mean_sq + norm_eps) * gain
    return normed * cosine + roll(normed, 64, 1) * sine


def swap_halves(values):
    keep = (iota((8, 128), 0) < 4) == (iota((8, 128), 1) < 64)
    tiles = []
    for j in range(values.shape[1] // 128):
        tile = values[:, j * 128 : (j + 1) * 128]
        tiles.append(jnp.where(keep, tile, roll(roll(tile, 64, 1), 4, 0)))
    return jnp.concatenate(tiles, axis=1)


def kernel(
    lengths_ref,
    q_hbm,
    gate_hbm,
    k_hbm,
    v_hbm,
    qg_hbm,
    kg_hbm,
    qn_hbm,
    gn_hbm,
    kn_hbm,
    vn_hbm,
    resid_hbm,
    wo_hbm,
    ng_hbm,
    wg_hbm,
    wu_hbm,
    wd_hbm,
    out_hbm,
    dec_hbm,
    keys,
    vals,
    bias,
    nq,
    nk,
    nv,
    ngate,
    selfw,
    fold,
    piece_out,
    piece_in,
    gathered,
    x1_out,
    x1_in,
    x2,
    xa,
    xb_out,
    xb_in,
    xc,
    cos_t,
    sin_t,
    gates,
    q_ref,
    gate_ref,
    k_ref,
    v_ref,
    qg_ref,
    kg_ref,
    qn_ref,
    gn_ref,
    kn_ref,
    vn_ref,
    resid_ref,
    wo_ref,
    ng_ref,
    wg_ref,
    wu_ref,
    wd_ref,
    out_ref,
    dec_ref,
    in_sem,
    s1_send,
    s1_recv,
    kv_send,
    kv_recv,
    x1_send,
    x1_recv,
    x2_send,
    x2_recv,
    xa_send,
    xa_recv,
    xb_send,
    xb_recv,
    xc_send,
    xc_recv,
    ring_send,
    ring_recv,
    out_sem,
):
    xlo, z, y = lax.axis_index("xlo"), lax.axis_index("z"), lax.axis_index("y")
    t = lax.axis_index("xhi") * 2 + lax.axis_index("core")
    p = xlo * NY + y

    def tp_dev(i):
        return {"xhi": i // 2, "core": i % 2}

    def plane_dev(i):
        return {"xlo": i // NY, "y": i % NY}

    def z_dev(i):
        return {"z": i % NZ}

    barrier = pltpu.get_barrier_semaphore()
    mesh_id = pl.DeviceIdType.MESH
    for d in range(1, NT):
        pl.semaphore_signal(barrier, inc=1, device_id=tp_dev((t + d) % NT), device_id_type=mesh_id)
    for d in range(1, NP):
        pl.semaphore_signal(barrier, inc=1, device_id=plane_dev((p + d) % NP), device_id_type=mesh_id)
    for d in (1, 2, NZ - 2, NZ - 1):
        pl.semaphore_signal(barrier, inc=1, device_id=z_dev(z + d), device_id_type=mesh_id)

    loads = {}
    for n, (name, src, dst) in enumerate(
        (
            ("wg", wg_hbm, wg_ref),
            ("wu", wu_hbm, wu_ref),
            ("wd", wd_hbm, wd_ref),
            ("k", k_hbm, k_ref),
            ("qg", qg_hbm, qg_ref),
            ("kg", kg_hbm, kg_ref),
            ("v", v_hbm, v_ref),
            ("qn", qn_hbm, qn_ref),
            ("kn", kn_hbm, kn_ref),
            ("vn", vn_hbm, vn_ref),
            ("gn", gn_hbm, gn_ref),
            ("resid", resid_hbm, resid_ref),
            ("gate", gate_hbm, gate_ref),
            ("wo", wo_hbm, wo_ref),
            ("ng", ng_hbm, ng_ref),
            ("q", q_hbm, q_ref),
        )
    ):
        loads[name] = pltpu.make_async_copy(src, dst, in_sem.at[n])
        loads[name].start()

    def arrive(*wanted):
        for name in wanted:
            loads[name].wait()

    started = []

    def send(src, dst, send_sem, recv_sem, device):
        copy = pltpu.make_async_remote_copy(
            src_ref=src,
            dst_ref=dst,
            send_sem=send_sem,
            recv_sem=recv_sem,
            device_id=device,
            device_id_type=mesh_id,
        )
        copy.start()
        started.append(copy)
        return copy

    arrive("wg", "wu", "wd")
    for n, ref in enumerate((wg_ref, wu_ref, wd_ref)):
        whole = ref[...].astype(f32)
        width = whole.shape[1]
        for i in range(NP):
            part = whole if i == 0 else roll(whole, width - CHUNK * i, 1)
            piece_out[i, :, n * 128 : (n + 1) * 128] = part[:, :128].astype(bf16)
    piece_in[pl.ds(p, 1)] = piece_out[pl.ds(p, 1)]

    len0, len1, len2 = lengths_ref[0, 0], lengths_ref[0, 1], lengths_ref[0, 2]
    end0, end1 = len0, len0 + len1
    end2 = end1 + len2

    def start_of(index):
        return jnp.where(index >= end1, end1, jnp.where(index >= end0, end0, 0))

    left = iota((TOK // 2, 128), 1) < 64
    own_index = t * TOK + iota((TOK // 2, 128), 0) + jnp.where(left, 0, TOK // 2)
    for ref, packed, sign in zip((cos_t, sin_t), angle_tables((own_index - start_of(own_index)).astype(f32)), (1.0, -1.0)):
        turned = roll(packed, 64, 1)
        ref[: TOK // 2, :] = jnp.where(left, sign * packed, turned)
        ref[TOK // 2 :, :] = jnp.where(left, sign * turned, packed)
    cosine, sine = cos_t[...], sin_t[...]

    arrive("k", "qg", "kg", "v")
    k_gain = kg_ref[...]
    q_gain = qg_ref[...]
    for k in range(KVH):
        lanes = slice(k * HD, (k + 1) * HD)
        keys[2, :, lanes] = norm_rope(k_ref[:, lanes].astype(f32), k_gain, cosine, sine).astype(bf16)
    arrive("qn", "kn", "vn", "gn")
    for ref in (nq, nk, nv, ngate):
        ref[...] = jnp.zeros_like(ref)
    for h in range(HEADS):
        rows = slice(h * 4, h * 4 + 3)
        lanes = slice(h * HD, (h + 1) * HD)
        kv_lanes = slice(h // 2 * HD, (h // 2 + 1) * HD)
        nq[rows, :] = qn_ref[:, lanes].astype(f32)
        nk[rows, :] = kn_ref[:, kv_lanes].astype(f32)
        nv[rows, :] = vn_ref[:, kv_lanes].astype(f32)
        ngate[rows, :] = jnp.broadcast_to(gn_ref[:, h : h + 1].astype(f32), (3, HD))
    request = iota((8, HD), 0) % 4
    new_pos = jnp.where(request == 0, len0, jnp.where(request == 1, len1, jnp.where(request == 2, len2, 0)))
    new_cos, new_sin = angle_tables(new_pos.astype(f32))
    new_sin = jnp.where(iota((8, HD), 1) < 64, -new_sin, new_sin)
    new_cos = jnp.concatenate([new_cos] * 4, axis=0)
    new_sin = jnp.concatenate([new_sin] * 4, axis=0)
    scale = HD**-0.5
    new_q = norm_rope(nq[...], q_gain, new_cos, new_sin).astype(bf16)
    new_k = norm_rope(nk[...], k_gain, new_cos, new_sin).astype(bf16)
    self_score = jnp.sum(new_q.astype(f32) * new_k.astype(f32), axis=-1, keepdims=True) * scale
    selfw[...] = jnp.broadcast_to(jnp.exp(self_score), selfw.shape)
    nq[...] = new_q.astype(f32)

    row_req = iota((8, TOK), 0) % 4
    token = t * TOK + iota((8, TOK), 1)
    begin = jnp.where(row_req == 0, 0, jnp.where(row_req == 1, end0, jnp.where(row_req == 2, end1, 0)))
    finish = jnp.where(row_req == 0, end0, jnp.where(row_req == 1, end1, jnp.where(row_req == 2, end2, 0)))
    own_bias = jnp.where((token >= begin) & (token < finish), 0.0, MASKED)
    for k in range(KVH):
        lanes = slice(k * HD, (k + 1) * HD)
        scores = nt_dot(nq[k * 8 : (k + 1) * 8, :].astype(bf16), keys[2, :, lanes]) * scale
        weights = jnp.exp(scores + own_bias)
        x1_out[k, 0:8, :] = jnp.dot(weights.astype(bf16), v_ref[:, lanes], preferred_element_type=f32)
        x1_out[k, 8:16, :] = jnp.broadcast_to(jnp.sum(weights, axis=-1, keepdims=True), (8, HD))
    x1_in[pl.ds(t, 1)] = x1_out[pl.ds(t, 1)]
    pl.semaphore_wait(barrier, NT - 1 + NP - 1 + 4)
    s1 = [
        send(piece_out.at[(p + d) % NP], piece_in.at[p], s1_send.at[d - 1], s1_recv.at[d - 1], plane_dev((p + d) % NP))
        for d in range(1, NP)
    ]

    c1 = [
        send(x1_out.at[(t + d) % NT], x1_in.at[t], x1_send.at[d - 1], x1_recv.at[d - 1], tp_dev((t + d) % NT))
        for d in range(1, NT)
    ]
    for d in (1, 2):

        @pl.when(t + d < NT)
        def _(d=d):
            for n, (src, dst) in enumerate(((keys.at[2], keys.at[2 - d]), (v_ref, vals.at[2 - d]))):
                pltpu.make_async_remote_copy(
                    src_ref=src,
                    dst_ref=dst,
                    send_sem=kv_send.at[d - 1, n],
                    recv_sem=kv_recv.at[d - 1, n],
                    device_id=tp_dev(lax.rem(t + d, NT)),
                    device_id_type=mesh_id,
                ).start()

        @pl.when(t < d)
        def _(d=d):
            keys[2 - d] = jnp.zeros((TOK, KVH * HD), bf16)
            vals[2 - d] = jnp.zeros((TOK, KVH * HD), bf16)


    for copy in s1:
        copy.wait_recv()
    block = piece_in[...].reshape(NP * 16, 3 * 128).astype(f32)
    for n in range(3):
        turned = jnp.transpose(block[:, n * 128 : (n + 1) * 128])
        gathered[pl.ds(z, 1), n * CHUNK : (n + 1) * CHUNK, :] = turned[:CHUNK, :].astype(bf16)[None]

    far = {}
    near = []

    def pass_on(step, chunk, backward):
        key = (step, chunk, backward)
        if step > 1:
            far[(step - 1, chunk, backward)].wait_recv()
        sign = NZ - 1 if backward else 1
        origin = (z + (NZ - sign) * 2 * (step - 1)) % NZ
        slot = gathered.at[origin, pl.ds(chunk * ROWS, ROWS)]
        for reach in (2, 1):
            if backward and step == 4 and reach == 2:
                continue
            n = (((step - 1) * CHUNKS + chunk) * 2 + int(backward)) * 2 + reach - 1
            copy = send(slot, slot, ring_send.at[n], ring_recv.at[n], z_dev(z + sign * reach))
            if reach == 2 and step < 4:
                far[key] = copy
            else:
                near.append((step, copy))

    def ring_step(step):
        for chunk in range(CHUNKS):
            for backward in (False, True):
                pass_on(step, chunk, backward)

    ring_step(1)

    arrive("resid", "gate")
    low = iota((8, 1024), 0) < 4
    fold[...] = jnp.zeros_like(fold)
    fold[0:3, :] = resid_ref[:, :1024].astype(f32)
    fold[4:7, :] = resid_ref[:, 1024:].astype(f32)
    key_index = (t - 2) * TOK + iota((TOK, 3 * TOK), 1)
    query_index = t * TOK + iota((TOK, 3 * TOK), 0)
    allowed = (key_index >= start_of(query_index)) & (key_index <= query_index)
    bias[...] = jnp.where(allowed, 0.0, MASKED)
    gate_rows = jax.nn.sigmoid(gate_ref[...].astype(f32))
    gates[...] = jnp.transpose(jnp.concatenate([gate_rows, jnp.zeros((120, TOK), f32)], axis=0))

    arrive("wo")
    for copy in c1:
        copy.wait_recv()
    both = x1_in[0] + x1_in[1] + x1_in[2] + x1_in[3]
    mine = pl.ds(pl.multiple_of(t * 8, 8), 8)
    own_self = selfw[mine, :]
    mixed = both[0:8] + own_self * nv[mine, :]
    attended = (mixed / (both[8:16] + own_self) * jax.nn.sigmoid(ngate[mine, :])).astype(bf16)
    first = jnp.dot(attended, wo_ref[0:HD, :], preferred_element_type=f32)
    second = jnp.dot(attended, wo_ref[HD : 2 * HD, :], preferred_element_type=f32)
    sums = first + roll(second, 4, 0)
    x2[pl.ds(t, 1)] = jnp.where(low, sums[:, :1024], roll(sums[:, 1024:], 4, 0)).astype(bf16)[None]
    c2 = [
        send(x2.at[t], x2.at[t], x2_send.at[d - 1], x2_recv.at[d - 1], tp_dev((t + d) % NT))
        for d in range(1, NT)
    ]
    for d in (1, 2):

        @pl.when(t >= d)
        def _(d=d):
            for n, (src, dst) in enumerate(((keys.at[2], keys.at[2 - d]), (v_ref, vals.at[2 - d]))):
                pltpu.make_async_remote_copy(
                    src_ref=src,
                    dst_ref=dst,
                    send_sem=kv_send.at[d - 1, n],
                    recv_sem=kv_recv.at[d - 1, n],
                    device_id=tp_dev(lax.rem(t + d, NT)),
                    device_id_type=mesh_id,
                ).wait_recv()

    arrive("q", "ng")
    def attend(h):
        lanes = slice(h * HD, (h + 1) * HD)
        kv_lanes = slice(h // 2 * HD, (h // 2 + 1) * HD)
        query = norm_rope(q_ref[:, lanes].astype(f32), q_gain, cos_t[...], sin_t[...]).astype(bf16)
        total = jnp.zeros((TOK, 1), f32)
        mixed = jnp.zeros((TOK, HD), f32)
        for b in range(3):
            scores = nt_dot(query, keys[b, :, kv_lanes]) * scale
            weights = jnp.exp(scores + bias[:, b * TOK : (b + 1) * TOK])
            total = total + jnp.sum(weights, axis=-1, keepdims=True)
            value = v_ref[:, kv_lanes] if b == 2 else vals[b, :, kv_lanes]
            mixed = mixed + jnp.dot(weights.astype(bf16), value, preferred_element_type=f32)
        out_ref[:, lanes] = (mixed / total * gates[:, h : h + 1]).astype(bf16)

    ring_step(2)
    attend(0)
    attend(1)

    for copy in c2:
        copy.wait_recv()
    attn = x2[0].astype(f32) + x2[1].astype(f32) + x2[2].astype(f32) + x2[3].astype(f32)
    hidden = fold[...] + attn
    squares = jnp.sum(hidden * hidden, axis=-1, keepdims=True)
    squares = jnp.broadcast_to(squares, (8, 128))
    mean_sq = ((squares + roll(squares, 4, 0)) / 2048.0)[:, 0:1]
    gain = jnp.where(low, ng_ref[:, :1024], ng_ref[:, 1024:])
    normed = hidden * lax.rsqrt(mean_sq + norm_eps) * gain
    xa[pl.ds(p, 1)] = swap_halves(normed).astype(bf16)[None]
    ca = [
        send(xa.at[p], xa.at[p], xa_send.at[d - 1], xa_recv.at[d - 1], plane_dev((p + d) % NP))
        for d in range(1, NP)
    ]
    ring_step(3)
    attend(2)
    attend(3)
    attend(4)
    ring_step(4)
    for h in range(5, HEADS):
        attend(h)
    result_copy = pltpu.make_async_copy(out_ref, out_hbm, out_sem.at[0])
    result_copy.start()

    for copy in ca:
        copy.wait_recv()

    def product(away):
        origin = (z + NZ + away) % NZ
        lanes = pl.ds(pl.multiple_of(origin // 2 * 128, 128), 128)
        tokens = xa[:, :, lanes].astype(f32).reshape(NP * 8, 128).astype(bf16)
        return nt_dot(tokens, gathered[pl.ds(origin, 1), 0 : 2 * CHUNK, :][0])

    same = product(0)
    for away in (2, -2, 4, -4):
        same = same + product(away)
    for step, copy in near:
        if step < 4:
            copy.wait_recv()
    other = product(1)
    for away in (-1, 3, -3, 5, -5):
        other = other + product(away)
    same = same + product(6) + product(-6)
    for step, copy in near:
        if step == 4:
            copy.wait_recv()
    same = same + product(8)
    other = other + product(7) + product(-7)
    fill = jnp.zeros((NP * 8, 256 - 2 * CHUNK), f32)
    same = jnp.concatenate([same, fill], axis=1)
    other = jnp.concatenate([other, fill], axis=1)
    swap = (iota((NP * 8, 256), 0) * 0 + z % 2) == 1
    sums = jnp.where(swap, other, same) + roll(jnp.where(swap, same, other), NP * 8 - 4, 0)
    unit_gate = sums[:, :CHUNK]
    unit_up = roll(sums, 256 - CHUNK, 1)[:, :CHUNK]
    units = (unit_gate / (1.0 + jnp.exp(-unit_gate)) * unit_up).astype(bf16)
    low_rows = iota((NP * 8, 128), 0) % 8 < 4
    for j in range(NZ // 2):
        even = jnp.dot(units, gathered[2 * j, 2 * CHUNK : 3 * CHUNK, :], preferred_element_type=f32)
        odd = jnp.dot(units, gathered[2 * j + 1, 2 * CHUNK : 3 * CHUNK, :], preferred_element_type=f32)
        xb_out[:, :, j * 128 : (j + 1) * 128] = jnp.where(low_rows, even, roll(odd, 4, 0)).reshape(NP, 8, 128).astype(bf16)
    xb_in[pl.ds(p, 1)] = xb_out[pl.ds(p, 1)]
    cb = [
        send(xb_out.at[(p + d) % NP], xb_in.at[p], xb_send.at[d - 1], xb_recv.at[d - 1], plane_dev((p + d) % NP))
        for d in range(1, NP)
    ]
    for copy in cb:
        copy.wait_recv()
    total = xb_in[0].astype(f32)
    for i in range(1, NP):
        total = total + xb_in[i].astype(f32)
    xc[pl.ds(t, 1)] = total.astype(bf16)[None]
    cc = [
        send(xc.at[t], xc.at[t], xc_send.at[d - 1], xc_recv.at[d - 1], tp_dev((t + d) % NT))
        for d in range(1, NT)
    ]
    for copy in cc:
        copy.wait_recv()
    down = xc[0].astype(f32) + xc[1].astype(f32) + xc[2].astype(f32) + xc[3].astype(f32)
    result = (hidden + swap_halves(down)).astype(bf16)
    dec_ref[:, :1024] = result[0:3]
    dec_ref[:, 1024:] = result[4:7]
    last_copy = pltpu.make_async_copy(dec_ref, dec_hbm, out_sem.at[1])
    last_copy.start()

    for copy in started:
        copy.wait_send()
    result_copy.wait()
    last_copy.wait()
    for d in (1, 2):

        @pl.when(t + d < NT)
        def _(d=d):
            for n, (src, dst) in enumerate(((keys.at[2], keys.at[2 - d]), (v_ref, vals.at[2 - d]))):
                pltpu.make_async_remote_copy(
                    src_ref=src,
                    dst_ref=dst,
                    send_sem=kv_send.at[d - 1, n],
                    recv_sem=kv_recv.at[d - 1, n],
                    device_id=tp_dev(lax.rem(t + d, NT)),
                    device_id_type=mesh_id,
                ).wait_send()


def local(
    q_pre,
    gate_pre,
    k_pre,
    v_pre,
    q_gain,
    k_gain,
    lengths,
    q_new,
    gate_new,
    k_new,
    v_new,
    resid,
    w_out,
    norm_gain,
    w_gate,
    w_up,
    w_down,
):
    dma = pltpu.SemaphoreType.DMA
    return pl.pallas_call(
        kernel,
        out_shape=(
            jax.ShapeDtypeStruct((TOK, HEADS * HD), bf16),
            jax.ShapeDtypeStruct((3, 2048), bf16),
        ),
        in_specs=[pl.BlockSpec(memory_space=pltpu.SMEM)] + [pl.BlockSpec(memory_space=pltpu.HBM)] * 16,
        out_specs=(pl.BlockSpec(memory_space=pltpu.HBM),) * 2,
        scratch_shapes=[
            pltpu.VMEM((3, TOK, KVH * HD), bf16),
            pltpu.VMEM((2, TOK, KVH * HD), bf16),
            pltpu.VMEM((TOK, 3 * TOK), f32),
            pltpu.VMEM((HEADS * 4, HD), f32),
            pltpu.VMEM((HEADS * 4, HD), f32),
            pltpu.VMEM((HEADS * 4, HD), f32),
            pltpu.VMEM((HEADS * 4, HD), f32),
            pltpu.VMEM((HEADS * 4, HD), f32),
            pltpu.VMEM((8, 1024), f32),
            pltpu.VMEM((NP, 16, 384), bf16),
            pltpu.VMEM((NP, 16, 384), bf16),
            pltpu.VMEM((NZ, 3 * CHUNK, 128), bf16),
            pltpu.VMEM((NT, 16, 128), f32),
            pltpu.VMEM((NT, 16, 128), f32),
            pltpu.VMEM((NT, 8, 1024), bf16),
            pltpu.VMEM((NP, 8, 1024), bf16),
            pltpu.VMEM((NP, 8, 1024), bf16),
            pltpu.VMEM((NP, 8, 1024), bf16),
            pltpu.VMEM((NT, 8, 1024), bf16),
            pltpu.VMEM((TOK, HD), f32),
            pltpu.VMEM((TOK, HD), f32),
            pltpu.VMEM((TOK, 128), f32),
            pltpu.VMEM((TOK, HEADS * HD), bf16),
            pltpu.VMEM((HEADS, TOK), bf16),
            pltpu.VMEM((TOK, KVH * HD), bf16),
            pltpu.VMEM((TOK, KVH * HD), bf16),
            pltpu.VMEM((1, HD), f32),
            pltpu.VMEM((1, HD), f32),
            pltpu.VMEM((3, HEADS * HD), bf16),
            pltpu.VMEM((3, HEADS), bf16),
            pltpu.VMEM((3, KVH * HD), bf16),
            pltpu.VMEM((3, KVH * HD), bf16),
            pltpu.VMEM((3, 2048), bf16),
            pltpu.VMEM((2 * HD, 2048), bf16),
            pltpu.VMEM((1, 2048), f32),
            pltpu.VMEM((16, 768), bf16),
            pltpu.VMEM((16, 768), bf16),
            pltpu.VMEM((16, 768), bf16),
            pltpu.VMEM((TOK, HEADS * HD), bf16),
            pltpu.VMEM((3, 2048), bf16),
            dma((16,)),
            dma((NP - 1,)),
            dma((NP - 1,)),
            dma((2, 2)),
            dma((2, 2)),
            dma((NT - 1,)),
            dma((NT - 1,)),
            dma((NT - 1,)),
            dma((NT - 1,)),
            dma((NP - 1,)),
            dma((NP - 1,)),
            dma((NP - 1,)),
            dma((NP - 1,)),
            dma((NT - 1,)),
            dma((NT - 1,)),
            dma((4 * CHUNKS * 4,)),
            dma((4 * CHUNKS * 4,)),
            dma((2,)),
        ],
        compiler_params=pltpu.CompilerParams(
            collective_id=0, has_side_effects=True, vmem_limit_bytes=60 * 1024 * 1024
        ),
    )(
        lengths,
        q_pre,
        gate_pre.T,
        k_pre,
        v_pre,
        q_gain.reshape(1, HD),
        k_gain.reshape(1, HD),
        q_new,
        gate_new,
        k_new,
        v_new,
        resid,
        w_out,
        norm_gain.reshape(1, 2048),
        w_gate,
        w_up,
        w_down.T,
    )


def solution(mesh):
    wide = jax.sharding.Mesh(
        mesh.devices.reshape(NX, NZ, NY, 2, 2), ("xlo", "z", "y", "xhi", "core")
    )
    return jax.shard_map(
        local,
        mesh=wide,
        in_specs=(
            P(req + tp, None),
            P(req + tp, None),
            P(req + tp, None),
            P(req + tp, None),
            P(),
            P(),
            P(req, None),
            P(req, None),
            P(req, None),
            P(req, None),
            P(req, None),
            P(req, None),
            P(tp, None),
            P(),
            P(req, tp),
            P(req, tp),
            P(tp, req),
        ),
        out_specs=(P(req + tp, None), P(req, None)),
        check_vma=False,
    )
```
